32 devices in a mesh: groups: 2 (over x), seq: 16 (over z, y, core).
Axes of the slice: x: 2, y: 2, z: 4, core: 2. Of those that a mesh axis runs over, the one named last changes fastest.
Arguments:
- seqs_in: bfloat16 [4, 4096, 1536], P('groups', 'seq'), parts along dimension 0, may hold values from -6 to 6
- pooled_grad: bfloat16 [4, 1024, 1536], P('groups', 'seq'), parts along dimension 0, may hold values from -6 to 6
- scale_in: float32 [1536], replicated, may hold values from 0.5 to 2
- shift_in: float32 [1536], replicated, may hold values from -3 to 3
- tap_weight_stack: bfloat16 [3, 1536, 768], replicated, may hold values from -0.09375 to 0.09375
- scale_mid: float32 [768], replicated, may hold values from 0.5 to 2
- shift_mid: float32 [768], replicated, may hold values from -3 to 3
- out_weight: bfloat16 [768, 1536], replicated, may hold values from -0.21875 to 0.21875
- out_bias: float32 [1536], replicated, may hold values from -3 to 3
Outputs:
- pooled: bfloat16 [4, 1024, 1536], P('groups', 'seq'), parts along dimension 0
- seq_grad: bfloat16 [4, 4096, 1536], P('groups', 'seq'), parts along dimension 0
The draws below stay inside these ranges and needn't reach their ends.
There are 2 independent parts, one for each index of `groups`. The reference program is written for one: setup_inputs(seed, part) draws one part's arguments, and reference() takes and returns one part's arrays. A program takes and returns all parts, laid end to end along the dimension named above; an argument that names none is the same for every part. Nothing has to cross between parts.
All inputs are finite; a program needn't handle non-finite values.
Results may differ from the reference program's by a relative error of at most 0.0051.
Values may be sent and summed in bfloat16 or wider, within the bound.
No kernel may reach another device: no remote copies, remote signals or barrier semaphores. Data moves between devices by JAX's collectives and lax.ppermute only.
A program may use at most 64 MiB of HBM per device.

```python
import math
import jax
import jax.numpy as jnp
from jax import lax

C = 1536
CH = 768
SEQS = 2
DILATION_STEP = 512
LEN = 4096
BINS = 1024


def shard_levels(rng, extent, pieces, least, high):
    gain = 1.0
    for axis_at, blocks in pieces:
        heights = jax.random.uniform(jax.random.fold_in(jax.random.fold_in(rng, 6), axis_at), (blocks,), jnp.float32, least / len(pieces), high / len(pieces))
        gain = gain * jnp.repeat(jnp.exp(heights), extent[axis_at] // blocks).reshape((-1,) + (1,) * (len(extent) - 1 - axis_at))
    return gain


def noise(rng, extent, deviation, bound, shards=(), kind=jnp.bfloat16):
    gain = shard_levels(rng, extent, shards, -0.22, 0.18) if shards else 1.0
    drawn = jax.random.normal(rng, extent, jnp.float32) * deviation * gain
    return jnp.minimum(jnp.maximum(drawn, -bound), bound).astype(kind)


def setup_inputs(seed: int = 0, part: int = 0) -> dict:
    seeds = jax.random.split(jax.random.key(seed), 10)
    part_splits = jax.random.split(jax.random.fold_in(seeds[9], part), 10)
    seqs_in = noise(part_splits[0], (SEQS, LEN, C), 1.0, 6.0, ((1, 16),))
    pooled_grad = noise(part_splits[1], (SEQS, BINS, C), 1.0, 6.0, ((1, 16),))
    scale_in = jnp.clip(jnp.exp(jax.random.uniform(seeds[2], (C,), jnp.float32, math.log(0.5), math.log(2.0))), 0.5, 2.0)
    shift_in = noise(seeds[3], (C,), 0.5, 3.0, (), jnp.float32)
    tap_weight_stack = noise(seeds[4], (3, C, CH), (3 * C) ** -0.5, 0.09375)
    scale_mid = jnp.clip(jnp.exp(jax.random.uniform(seeds[5], (CH,), jnp.float32, math.log(0.5), math.log(2.0))), 0.5, 2.0)
    shift_mid = noise(seeds[6], (CH,), 0.5, 3.0, (), jnp.float32)
    out_weight = noise(seeds[7], (CH, C), CH ** -0.5, 0.21875)
    out_bias = noise(seeds[8], (C,), 0.5, 3.0, (), jnp.float32)
    return dict(seqs_in=seqs_in, pooled_grad=pooled_grad, scale_in=scale_in, shift_in=shift_in, tap_weight_stack=tap_weight_stack, scale_mid=scale_mid, shift_mid=shift_mid, out_weight=out_weight, out_bias=out_bias)


gelu_coef = 0.7978845608028654


def gelu_value(v):
    inner = jnp.tanh(gelu_coef * (v + 0.044715 * v * v * v))
    return 0.5 * v * (1.0 + inner)


def gelu_slope(v):
    inner = jnp.tanh(gelu_coef * (v + 0.044715 * v * v * v))
    return 0.5 * (1.0 + inner) + 0.5 * v * (1.0 - inner * inner) * gelu_coef * (1.0 + 0.134145 * v * v)


def shift_row_blocks(value, offset):
    blank = jnp.zeros_like(value[:, :abs(offset)])
    if offset > 0:
        return jnp.concatenate([blank, value[:, :-offset]], axis=1)
    return jnp.concatenate([value[:, -offset:], blank], axis=1)


def product_over_rows(value, weight):
    flat = value.reshape(-1, value.shape[-1])
    prod = jnp.dot(flat, weight, preferred_element_type=jnp.float32)
    return prod.reshape(value.shape[:-1] + (weight.shape[1],))


def product_backward(value, weight):
    flat = value.reshape(-1, value.shape[-1])
    prod = lax.dot_general(flat, weight, (((1,), (1,)), ((), ())), preferred_element_type=jnp.float32)
    return prod.reshape(value.shape[:-1] + (weight.shape[0],))


def reference(seqs_in, pooled_grad, scale_in, shift_in, tap_weight_stack, scale_mid, shift_mid, out_weight, out_bias):
    xfull = seqs_in.astype(jnp.float32)
    first = xfull * scale_in + shift_in
    layer_activations = gelu_value(first).astype(jnp.bfloat16)
    middle_state = product_over_rows(shift_row_blocks(layer_activations, DILATION_STEP), tap_weight_stack[0]) + product_over_rows(layer_activations, tap_weight_stack[1]) + product_over_rows(shift_row_blocks(layer_activations, -DILATION_STEP), tap_weight_stack[2])
    second = middle_state * scale_mid + shift_mid
    hidden = gelu_value(second).astype(jnp.bfloat16)
    block_out = (xfull + product_over_rows(hidden, out_weight) + out_bias).astype(jnp.bfloat16)
    block_wide = lax.optimization_barrier(block_out).astype(jnp.float32)
    pooled = jnp.mean(block_wide.reshape(block_wide.shape[0], -1, 4, block_wide.shape[2]), axis=2).astype(jnp.bfloat16)
    out_grad = (jnp.repeat(pooled_grad, 4, axis=1).astype(jnp.float32) * 0.25).astype(jnp.bfloat16)
    hidden_grad = product_backward(out_grad, out_weight)
    middle_gradient = (hidden_grad * gelu_slope(second) * scale_mid).astype(jnp.bfloat16)
    activation_gradient = product_backward(shift_row_blocks(middle_gradient, -DILATION_STEP), tap_weight_stack[0]) + product_backward(middle_gradient, tap_weight_stack[1]) + product_backward(shift_row_blocks(middle_gradient, DILATION_STEP), tap_weight_stack[2])
    seq_grad = (out_grad.astype(jnp.float32) + activation_gradient * gelu_slope(first) * scale_in).astype(jnp.bfloat16)
    return (pooled, seq_grad)
```

```python
import functools

import jax
import jax.numpy as jnp
from jax import lax
from jax.experimental import pallas as pl
from jax.experimental.pallas import tpu as pltpu
from jax.sharding import PartitionSpec as P

DILATION_STEP = 512
BIN = 4
LANES = 128
AXIS = "seq"
GELU_COEF = 0.7978845608028654
F32 = jnp.float32
BF16 = jnp.bfloat16
LIMIT = 12 * 1024 * 1024


def gelu_value(v):
    inner = jnp.tanh(v * (GELU_COEF + (GELU_COEF * 0.044715) * v * v))
    half = 0.5 * v
    return half + half * inner


def gelu_both(v):
    square = v * v
    inner = jnp.tanh(v * (GELU_COEF + (GELU_COEF * 0.044715) * square))
    half = 0.5 * v
    value = half + half * inner
    slope = (0.5 + 0.5 * inner) + half * (1.0 - inner * inner) * (
        GELU_COEF + (GELU_COEF * 0.134145) * square
    )
    return value, slope


def gelu_slope(v):
    return gelu_both(v)[1]


def dot_nn(a, b):
    return jnp.dot(a, b, preferred_element_type=F32)


def dot_nt(a, b):
    return lax.dot_general(a, b, (((1,), (1,)), ((), ())), preferred_element_type=F32)


def averaging(bins, rows):
    row = lax.broadcasted_iota(jnp.int32, (bins, rows), 0)
    column = lax.broadcasted_iota(jnp.int32, (bins, rows), 1)
    inside = (column >= row * BIN) & (column < row * BIN + BIN)
    return jnp.where(inside, 1.0 / BIN, 0.0).astype(BF16)


def spreading(rows, bins):
    row = lax.broadcasted_iota(jnp.int32, (rows, bins), 0)
    column = lax.broadcasted_iota(jnp.int32, (rows, bins), 1)
    inside = (row >= column * BIN) & (row < column * BIN + BIN)
    return jnp.where(inside, 1.0 / BIN, 0.0).astype(BF16)


def near_tap(stride):
    return 2 * lax.rem(lax.div(lax.axis_index(AXIS), stride), 2)


def local_call(body, name, operands, outs, cost, scratch=()):
    flops, nbytes, trans = cost
    single = not isinstance(outs, list)
    space = pl.BlockSpec(memory_space=pltpu.VMEM)
    shapes = [pltpu.VMEM(s, d) for s, d in ([outs] if single else outs)]
    return pl.pallas_call(
        body,
        name=name,
        in_specs=[space] * len(operands),
        out_specs=space if single else [space] * len(outs),
        out_shape=shapes[0] if single else shapes,
        scratch_shapes=list(scratch),
        compiler_params=pltpu.CompilerParams(vmem_limit_bytes=LIMIT),
        cost_estimate=pl.CostEstimate(flops=flops, bytes_accessed=nbytes, transcendentals=trans),
    )(*[pltpu.with_memory_space_constraint(v, pltpu.VMEM) for v in operands])


def front_two_body(which, x_ref, s_ref, b_ref, w_ref, a_ref, p_ref, q_ref):
    a_ref[...] = gelu_value(x_ref[which].astype(F32) * s_ref[...] + b_ref[...]).astype(BF16)
    p_ref[...] = dot_nn(a_ref[...], w_ref[0]).astype(BF16)
    q_ref[...] = dot_nn(a_ref[...], w_ref[2]).astype(BF16)


def front_two(x, which, scale, shift, taps):
    _, rows, width = x.shape
    mid = taps.shape[2]
    return local_call(
        functools.partial(front_two_body, which),
        "front_two",
        [x, scale, shift, taps],
        [((rows, width), BF16), ((rows, mid), BF16), ((rows, mid), BF16)],
        (4 * rows * width * mid, 4 * rows * width, rows * width),
    )


def front_one_body(which, stride, x_ref, s_ref, b_ref, w_ref, a_ref, p_ref):
    a_ref[...] = gelu_value(x_ref[which].astype(F32) * s_ref[...] + b_ref[...]).astype(BF16)
    p_ref[...] = dot_nn(a_ref[...], w_ref[2 - near_tap(stride)]).astype(BF16)


def front_one(x, which, scale, shift, taps, stride):
    _, rows, width = x.shape
    mid = taps.shape[2]
    return local_call(
        functools.partial(front_one_body, which, stride),
        "front_one",
        [x, scale, shift, taps],
        [((rows, width), BF16), ((rows, mid), BF16)],
        (2 * rows * width * mid, 4 * rows * width, rows * width),
    )


def centre_body(stride, a_ref, b_ref, w_ref, p_ref, q_ref, k_ref):
    k_ref[...] = dot_nn(b_ref[...], w_ref[near_tap(stride)])
    p_ref[...] = dot_nn(a_ref[...], w_ref[1])
    q_ref[...] = dot_nn(b_ref[...], w_ref[1])


def centre(a, b, taps, stride):
    rows, width = a.shape
    mid = taps.shape[2]
    return local_call(
        functools.partial(centre_body, stride),
        "centre",
        [a, b, taps],
        [((rows, mid), F32)] * 3,
        (6 * rows * width * mid, 4 * rows * width, 0),
    )


def join_body(k_ref, r_ref, o_ref):
    o_ref[...] = (k_ref[...] + r_ref[...].astype(F32)).astype(BF16)


def join(kept, came):
    return local_call(
        join_body, "join", [kept, came], (kept.shape, BF16), (kept.size, 8 * kept.size, 0)
    )


def hidden_grad_body(g_ref, w_ref, o_ref):
    for n in range(g_ref.shape[0]):
        o_ref[n] = dot_nt((g_ref[n].astype(F32) * (1.0 / BIN)).astype(BF16), w_ref[...])


def hidden_grad(binned, weight):
    batch, bins, width = binned.shape
    mid = weight.shape[0]
    return local_call(
        hidden_grad_body,
        "hidden_grad",
        [binned, weight],
        ((batch, bins, mid), F32),
        (2 * batch * bins * width * mid, 2 * batch * bins * width, 0),
    )


def middle_body(count, which, *refs):
    parts = refs[:count]
    p_ref, s_ref, b_ref, hg_ref, g_ref, h_ref, wide_ref = refs[count:]
    _, bins, width = hg_ref.shape
    for lane in range(width // LANES):
        columns = slice(lane * LANES, lane * LANES + LANES)
        for k in range(BIN):
            wide_ref[lane, pl.ds(k, bins, stride=BIN), :] = hg_ref[which, :, columns]
    scales, shifts = s_ref[...].reshape(1, width), b_ref[...].reshape(1, width)
    for lane in range(width // LANES):
        columns = slice(lane * LANES, lane * LANES + LANES)
        mid = p_ref[:, columns]
        for part in parts:
            mid = mid + part[:, columns].astype(F32)
        scale = scales[:, columns]
        value, slope = gelu_both(mid * scale + shifts[:, columns])
        g_ref[:, columns] = (wide_ref[lane] * slope * scale).astype(BF16)
        h_ref[:, columns] = value.astype(BF16)


def middle(parts, centre_part, which, scale, shift, hidden_grads):
    rows, mid = centre_part.shape
    return local_call(
        functools.partial(middle_body, len(parts), which),
        "middle",
        [*parts, centre_part, scale, shift, hidden_grads],
        [((rows, mid), BF16), ((rows, mid), BF16)],
        (30 * rows * mid, 12 * rows * mid, rows * mid),
        scratch=[pltpu.VMEM((mid // LANES, rows, LANES), F32)],
    )


def pooled_body(count, *refs):
    hidden = refs[:count]
    x_ref, w_ref, b_ref, o_ref = refs[count:]
    _, bins, width = o_ref.shape
    average = averaging(bins, x_ref.shape[1])
    for n in range(count):
        mean = dot_nn(average, hidden[n][...]).astype(BF16)
        o_ref[n] = (
            dot_nn(average, x_ref[n]) + dot_nn(mean, w_ref[...]) + b_ref[...]
        ).astype(BF16)


def pooled_out(x, hidden, weight, bias):
    batch, rows, width = x.shape
    bins = rows // BIN
    mid = weight.shape[0]
    return local_call(
        functools.partial(pooled_body, batch),
        "pooled",
        [*hidden, x, weight, bias],
        ((batch, bins, width), BF16),
        (2 * batch * bins * width * (mid + rows), 2 * batch * rows * width, 0),
    )


def back_first_body(g_ref, w_ref, o_ref):
    o_ref[...] = dot_nt(g_ref[...], w_ref[1])


def back_first(g, taps):
    rows, mid = g.shape
    width = taps.shape[1]
    return local_call(
        back_first_body,
        "back_first",
        [g, taps],
        ((rows, width), F32),
        (2 * rows * width * mid, 4 * rows * width, 0),
    )


def back_near_body(stride, c_ref, g_ref, w_ref, o_ref):
    o_ref[...] = c_ref[...] + dot_nt(g_ref[...], w_ref[near_tap(stride)])


def back_near(total, g, taps, stride):
    rows, mid = g.shape
    width = taps.shape[1]
    return local_call(
        functools.partial(back_near_body, stride),
        "back_near",
        [total, g, taps],
        ((rows, width), F32),
        (2 * rows * width * mid, 8 * rows * width, 0),
    )


def final_body(count, which, stride, tiles, *refs):
    grads = refs[:count]
    c_ref, w_ref, x_ref, og_ref, s_ref, b_ref, _, o_ref, out_ref, sems = refs[count:]
    rows, width = c_ref.shape
    tile = width // tiles
    spread = spreading(rows, og_ref.shape[1])
    scales, shifts = s_ref[...].reshape(1, width), b_ref[...].reshape(1, width)
    taps = [2 - near_tap(stride)] if count == 1 else [0, 2]
    copies = []
    for n in range(tiles):
        columns = slice(n * tile, n * tile + tile)
        total = c_ref[:, columns]
        for g, tap in zip(grads, taps):
            total = total + dot_nt(g[...], w_ref[tap, columns, :])
        scale = scales[:, columns]
        slope = gelu_slope(x_ref[which, :, columns].astype(F32) * scale + shifts[:, columns])
        out_ref[:, columns] = (
            dot_nn(spread, og_ref[which, :, columns]) + total * slope * scale
        ).astype(BF16)
        copy = pltpu.make_async_copy(
            out_ref.at[:, columns], o_ref.at[which, :, columns], sems.at[n]
        )
        copy.start()
        copies.append(copy)
    for copy in copies:
        copy.wait()


def final(total, grads, taps, x, binned, which, scale, shift, stride, onto):
    batch, rows, width = x.shape
    mid = taps.shape[2]
    tiles = 3
    count = len(grads)
    operands = [*grads, total, taps, x, binned, scale, shift]
    space = pl.BlockSpec(memory_space=pltpu.VMEM)
    anywhere = pl.BlockSpec(memory_space=pltpu.HBM)
    operands = [pltpu.with_memory_space_constraint(v, pltpu.VMEM) for v in operands]
    specs = [space] * len(operands)
    body = functools.partial(final_body, count, which, stride, tiles)
    if onto is None:
        full = body
        body = lambda *refs: full(*refs[: len(specs)], None, *refs[len(specs) :])
        aliases = {}
        in_specs = specs
    else:
        aliases = {len(operands): 0}
        operands = operands + [onto]
        in_specs = specs + [anywhere]
    return pl.pallas_call(
        body,
        name="final",
        in_specs=in_specs,
        out_specs=anywhere,
        out_shape=jax.ShapeDtypeStruct((batch, rows, width), BF16),
        scratch_shapes=[pltpu.VMEM((rows, width), BF16), pltpu.SemaphoreType.DMA((tiles,))],
        input_output_aliases=aliases,
        compiler_params=pltpu.CompilerParams(vmem_limit_bytes=LIMIT),
        cost_estimate=pl.CostEstimate(
            flops=2 * count * rows * width * mid,
            bytes_accessed=8 * rows * width,
            transcendentals=rows * width,
        ),
    )(*operands)


def local(
    seqs_in,
    pooled_grad,
    scale_in,
    shift_in,
    tap_weight_stack,
    scale_mid,
    shift_mid,
    out_weight,
    out_bias,
):
    rows = seqs_in.shape[1]
    count = lax.axis_size(AXIS)
    stride = DILATION_STEP // rows
    blocks = count // stride
    taps = tap_weight_stack

    def hop(value, steps):
        return lax.ppermute(
            value, AXIS, [(i, i + steps) for i in range(count) if 0 <= i + steps < count]
        )

    def block_permute(value, move):
        pairs = []
        for b in range(blocks):
            to = move(b)
            if 0 <= to < blocks:
                pairs += [(b * stride + i, to * stride + i) for i in range(stride)]
        return lax.ppermute(value, AXIS, pairs)

    def swap(value):
        return block_permute(value, lambda b: b ^ 1)

    def inward(value):
        return block_permute(value, lambda b: b + 2 if b % 2 else b - 2)

    def outward(value):
        return block_permute(value, lambda b: b - 2 if b % 2 else b + 2)

    act0, first0, last0 = front_two(seqs_in, 0, scale_in, shift_in, taps)
    from_before0 = hop(first0, stride)
    from_after0 = hop(last0, -stride)
    act1, sent1 = front_one(seqs_in, 1, scale_in, shift_in, taps, stride)
    came1 = inward(sent1)
    centre0, centre1, kept1 = centre(act0, act1, taps, stride)
    hg = hidden_grad(pooled_grad, out_weight)
    both1 = swap(join(kept1, came1))
    grad0, hid0 = middle([from_before0, from_after0], centre0, 0, scale_mid, shift_mid, hg)
    near0 = swap(grad0)
    total0 = back_first(grad0, taps)
    grad1, hid1 = middle([both1], centre1, 1, scale_mid, shift_mid, hg)
    g_before1 = hop(grad1, stride)
    g_after1 = hop(grad1, -stride)
    far0 = outward(near0)
    total1 = back_first(grad1, taps)
    pooled = pooled_out(seqs_in, [hid0, hid1], out_weight, out_bias)
    total0 = back_near(total0, near0, taps, stride)
    grads = final(
        total0, [far0], taps, seqs_in, pooled_grad, 0, scale_in, shift_in, stride, None
    )
    grads = final(
        total1,
        [g_after1, g_before1],
        taps,
        seqs_in,
        pooled_grad,
        1,
        scale_in,
        shift_in,
        stride,
        grads,
    )
    return pooled, grads


def solution(mesh):
    in_specs = (
        P("groups", "seq", None),
        P("groups", "seq", None),
        P(),
        P(),
        P(),
        P(),
        P(),
        P(),
        P(),
    )
    out_specs = (P("groups", "seq", None), P("groups", "seq", None))
    return jax.shard_map(local, mesh=mesh, in_specs=in_specs, out_specs=out_specs, check_vma=False)
```

```python
import functools

import jax
import jax.numpy as jnp
from jax import lax
from jax.experimental import pallas as pl
from jax.experimental.pallas import tpu as pltpu
from jax.sharding import PartitionSpec as P

DILATION_STEP = 512
BIN = 4
LANES = 128
AXIS = "seq"
GELU_COEF = 0.7978845608028654
F32 = jnp.float32
BF16 = jnp.bfloat16
SHARE = 64
LIMIT = 12 * 1024 * 1024


def gelu_value(v):
    inner = jnp.tanh(v * (GELU_COEF + (GELU_COEF * 0.044715) * v * v))
    half = 0.5 * v
    return half + half * inner


def gelu_both(v):
    square = v * v
    inner = jnp.tanh(v * (GELU_COEF + (GELU_COEF * 0.044715) * square))
    half = 0.5 * v
    value = half + half * inner
    slope = (0.5 + 0.5 * inner) + half * (1.0 - inner * inner) * (
        GELU_COEF + (GELU_COEF * 0.134145) * square
    )
    return value, slope


def gelu_slope(v):
    return gelu_both(v)[1]


def dot_nn(a, b):
    return jnp.dot(a, b, preferred_element_type=F32)


def dot_nt(a, b):
    return lax.dot_general(a, b, (((1,), (1,)), ((), ())), preferred_element_type=F32)


def averaging(bins, rows):
    row = lax.broadcasted_iota(jnp.int32, (bins, rows), 0)
    column = lax.broadcasted_iota(jnp.int32, (bins, rows), 1)
    inside = (column >= row * BIN) & (column < row * BIN + BIN)
    return jnp.where(inside, 1.0 / BIN, 0.0).astype(BF16)


def spreading(rows, bins):
    row = lax.broadcasted_iota(jnp.int32, (rows, bins), 0)
    column = lax.broadcasted_iota(jnp.int32, (rows, bins), 1)
    inside = (row >= column * BIN) & (row < column * BIN + BIN)
    return jnp.where(inside, 1.0 / BIN, 0.0).astype(BF16)


def near_tap(stride):
    return 2 * lax.rem(lax.div(lax.axis_index(AXIS), stride), 2)


def cost_of(flops, nbytes, trans):
    return pl.CostEstimate(
        flops=flops // SHARE, bytes_accessed=nbytes // SHARE, transcendentals=trans // SHARE
    )


def local_call(body, name, operands, outs, cost, scratch=(), after=()):
    flops, nbytes, trans = cost
    single = not isinstance(outs, list)
    space = pl.BlockSpec(memory_space=pltpu.VMEM)
    if after:
        inner, skip = body, len(operands)
        body = lambda *refs: inner(*refs[:skip], *refs[skip + len(after) :])
        operands = [*operands, *after]
    shapes = [pltpu.VMEM(s, d) for s, d in ([outs] if single else outs)]
    return pl.pallas_call(
        body,
        name=name,
        in_specs=[space] * len(operands),
        out_specs=space if single else [space] * len(outs),
        out_shape=shapes[0] if single else shapes,
        scratch_shapes=list(scratch),
        compiler_params=pltpu.CompilerParams(vmem_limit_bytes=LIMIT),
        cost_estimate=cost_of(flops, nbytes, trans),
    )(*[pltpu.with_memory_space_constraint(v, pltpu.VMEM) for v in operands])

SPLITS = (256, 256, 256)


def bounds(n):
    return slice(sum(SPLITS[:n]), sum(SPLITS[: n + 1]))


def front_body(stride, x_hbm, s_hbm, b_hbm, w_hbm, x_ref, w_ref, a_ref, p_ref, s_ref, b_ref, sems):
    rows, width = x_ref.shape
    slabs = 4
    slab = rows // slabs
    copies = [
        pltpu.make_async_copy(s_hbm, s_ref, sems.at[0]),
        pltpu.make_async_copy(b_hbm, b_ref, sems.at[1]),
    ]
    copies += [
        pltpu.make_async_copy(
            x_hbm.at[pl.ds(n * slab, slab)], x_ref.at[pl.ds(n * slab, slab)], sems.at[2 + n]
        )
        for n in range(slabs)
    ]
    taps = pltpu.make_async_copy(w_hbm.at[2 - near_tap(stride)], w_ref, sems.at[2 + slabs])
    for copy in copies:
        copy.start()
    taps.start()
    copies[0].wait()
    copies[1].wait()
    scale = s_ref[...].reshape(1, width)
    shift = b_ref[...].reshape(1, width)
    for n, copy in enumerate(copies[2:]):
        copy.wait()
        part = slice(n * slab, n * slab + slab)
        a_ref[part, :] = gelu_value(x_ref[part, :].astype(F32) * scale + shift).astype(BF16)
    taps.wait()
    p_ref[...] = dot_nn(a_ref[...], w_ref[:, bounds(0)]).astype(BF16)


def front(x, scale, shift, taps, stride):
    rows, width = x.shape
    mid = SPLITS[0]
    space = pl.BlockSpec(memory_space=pltpu.VMEM)
    far = pl.BlockSpec(memory_space=pltpu.HBM)
    operands = [pltpu.with_memory_space_constraint(v, pltpu.HBM) for v in (x, scale, shift, taps)]
    return pl.pallas_call(
        functools.partial(front_body, stride),
        name="front",
        in_specs=[far] * 4,
        out_specs=[space] * 4,
        out_shape=[
            pltpu.VMEM(x.shape, BF16),
            pltpu.VMEM(taps.shape[1:], BF16),
            pltpu.VMEM((rows, width), BF16),
            pltpu.VMEM((rows, mid), BF16),
        ],
        scratch_shapes=[
            pltpu.VMEM((width,), F32),
            pltpu.VMEM((width,), F32),
            pltpu.SemaphoreType.DMA((7,)),
        ],
        compiler_params=pltpu.CompilerParams(vmem_limit_bytes=LIMIT),
        cost_estimate=cost_of(2 * rows * width * mid, 2 * (x.size + taps.size), x.size),
    )(*operands)


def side_body(which, a_ref, w_ref, o_ref):
    o_ref[...] = dot_nn(a_ref[...], w_ref[:, bounds(which)]).astype(BF16)


def side(act, far_tap, which, after=()):
    rows, width = act.shape
    return local_call(
        functools.partial(side_body, which),
        "side",
        [act, far_tap],
        ((rows, SPLITS[which]), BF16),
        (2 * rows * width * SPLITS[which], 2 * rows * width, 0),
        after=after,
    )


def keep_body(stride, which, a_ref, w_ref, *outs):
    for n, out in zip(which, outs):
        out[...] = dot_nn(a_ref[...], w_ref[near_tap(stride), :, bounds(n)])


def keep(act, taps, which, stride, after=()):
    rows, width = act.shape
    return local_call(
        functools.partial(keep_body, stride, which),
        "keep",
        [act, taps],
        [((rows, SPLITS[n]), F32) for n in which],
        (2 * rows * width * sum(SPLITS[n] for n in which), 2 * rows * width, 0),
        after=after,
    )


def centre_body(a_ref, w_ref, *outs):
    for n, out in enumerate(outs):
        out[...] = dot_nn(a_ref[...], w_ref[1, :, bounds(n)])


def centre(act, taps, after):
    rows, width = act.shape
    return local_call(
        centre_body,
        "centre",
        [act, taps],
        [((rows, c), F32) for c in SPLITS],
        (2 * rows * width * sum(SPLITS), 2 * rows * width, 0),
        after=after,
    )


def join_body(k_ref, r_ref, o_ref):
    o_ref[...] = (k_ref[...] + r_ref[...].astype(F32)).astype(BF16)


def join(kept, came, after=()):
    return local_call(
        join_body,
        "join",
        [kept, came],
        (kept.shape, BF16),
        (kept.size, 8 * kept.size, 0),
        after=after,
    )


def hidden_grad_body(g_ref, w_ref, *outs):
    grad = (g_ref[...].astype(F32) * (1.0 / BIN)).astype(BF16)
    for n, out in enumerate(outs):
        out[...] = dot_nt(grad, w_ref[bounds(n), :])


def hidden_grad(binned, weight, after):
    bins, width = binned.shape
    mid = weight.shape[0]
    return local_call(
        hidden_grad_body,
        "hidden_grad",
        [binned, weight],
        [((bins, c), F32) for c in SPLITS],
        (2 * bins * width * mid, 2 * bins * width, 0),
        after=after,
    )


def middle_body(which, t_ref, p_ref, s_ref, b_ref, hg_ref, g_ref, h_ref, wide_ref):
    bins, width = hg_ref.shape
    for lane in range(width // LANES):
        columns = slice(lane * LANES, lane * LANES + LANES)
        for k in range(BIN):
            wide_ref[lane, pl.ds(k, bins, stride=BIN), :] = hg_ref[:, columns]
    first = bounds(which).start
    scales = s_ref[...].reshape(1, s_ref.shape[0])
    shifts = b_ref[...].reshape(1, b_ref.shape[0])
    for lane in range(width // LANES):
        columns = slice(lane * LANES, lane * LANES + LANES)
        among = slice(first + lane * LANES, first + lane * LANES + LANES)
        mid = p_ref[:, columns] + t_ref[:, columns].astype(F32)
        scale = scales[:, among]
        value, slope = gelu_both(mid * scale + shifts[:, among])
        g_ref[:, columns] = (wide_ref[lane] * slope * scale).astype(BF16)
        h_ref[:, columns] = value.astype(BF16)


def middle(part, centre_part, which, scale, shift, hidden_grads, after=()):
    rows, mid = centre_part.shape
    return local_call(
        functools.partial(middle_body, which),
        "middle",
        [part, centre_part, scale, shift, hidden_grads],
        [((rows, mid), BF16), ((rows, mid), BF16)],
        (30 * rows * mid, 12 * rows * mid, rows * mid),
        scratch=[pltpu.VMEM((mid // LANES, rows, LANES), F32)],
        after=after,
    )


def pooled_base_body(x_ref, b_ref, o_ref):
    bins, width = o_ref.shape
    average = averaging(bins, x_ref.shape[0])
    o_ref[...] = dot_nn(average, x_ref[...]) + b_ref[...].reshape(1, width)


def pooled_base(x, bias, after):
    rows, width = x.shape
    bins = rows // BIN
    return local_call(
        pooled_base_body,
        "pooled_base",
        [x, bias],
        ((bins, width), F32),
        (2 * bins * width * rows, 2 * rows * width, 0),
        after=after,
    )


def pooled_body(*refs):
    count = len(SPLITS)
    hidden = refs[:count]
    base_ref, w_ref, o_ref, out_ref, sem = refs[count:]
    bins, width = out_ref.shape
    rows = hidden[0].shape[0]
    average = averaging(bins, rows)
    total = base_ref[...]
    for n in range(count):
        mean = dot_nn(average, hidden[n][...]).astype(BF16)
        total = total + dot_nn(mean, w_ref[bounds(n), :])
    out_ref[...] = total.astype(BF16)
    half = bins // o_ref.shape[0]
    for n in range(o_ref.shape[0]):
        copy = pltpu.make_async_copy(out_ref.at[pl.ds(n * half, half)], o_ref.at[n], sem.at[n])
        copy.start()
    for n in range(o_ref.shape[0]):
        copy = pltpu.make_async_copy(out_ref.at[pl.ds(n * half, half)], o_ref.at[n], sem.at[n])
        copy.wait()


def pooled_out(base, hidden, weight, batch):
    bins, width = base.shape
    mid = weight.shape[0]
    operands = [*hidden, base, weight]
    return pl.pallas_call(
        pooled_body,
        name="pooled",
        in_specs=[pl.BlockSpec(memory_space=pltpu.VMEM)] * len(operands),
        out_specs=pl.BlockSpec(memory_space=pltpu.HBM),
        out_shape=pltpu.HBM((batch, bins // batch, width), BF16),
        scratch_shapes=[pltpu.VMEM((bins, width), BF16), pltpu.SemaphoreType.DMA((batch,))],
        compiler_params=pltpu.CompilerParams(vmem_limit_bytes=LIMIT),
        cost_estimate=cost_of(2 * bins * width * mid, 6 * bins * width, 0),
    )(*[pltpu.with_memory_space_constraint(v, pltpu.VMEM) for v in operands])


def slope_body(x_ref, s_ref, b_ref, o_ref):
    width = x_ref.shape[1]
    scale = s_ref[...].reshape(1, width)
    shift = b_ref[...].reshape(1, width)
    o_ref[...] = gelu_slope(x_ref[...].astype(F32) * scale + shift) * scale


def slope_in(x, scale, shift, after):
    return local_call(
        slope_body,
        "slope",
        [x, scale, shift],
        (x.shape, F32),
        (30 * x.size, 6 * x.size, x.size),
        after=after,
    )


def back_sum(stride, refs, kinds, w_ref, columns=slice(None)):
    near = near_tap(stride)
    taps = dict(own=1, near=near, far=2 - near, before=2, later=0)
    total = None
    for ref, (kind, n) in zip(refs, kinds):
        term = dot_nt(ref[...], w_ref[taps[kind], columns, bounds(n)])
        total = term if total is None else total + term
    return total


def back_body(stride, kinds, started, *refs):
    grads = refs[: len(kinds)]
    rest = refs[len(kinds) :]
    w_ref, o_ref = rest[0], rest[-1]
    total = back_sum(stride, grads, kinds, w_ref)
    o_ref[...] = rest[1][...] + total if started else total


def back(total, terms, taps, stride, after=()):
    kinds = [(kind, n) for kind, n, _ in terms]
    grads = [g for _, _, g in terms]
    rows = grads[0].shape[0]
    width = taps.shape[1]
    started = total is not None
    return local_call(
        functools.partial(back_body, stride, kinds, started),
        "back",
        [*grads, taps] + ([total] if started else []),
        ((rows, width), F32),
        (2 * rows * width * sum(g.shape[1] for g in grads), 8 * rows * width, 0),
        after=after,
    )


def touch_body(a_ref, b_ref, o_ref):
    o_ref[...] = a_ref[:16, :LANES] + b_ref[:16, :LANES]


def touch(a, b):
    return local_call(touch_body, "touch", [a, b], ((16, LANES), BF16), (1, 1, 0))


def final_body(stride, kinds, tiles, *refs):
    grads = refs[: len(kinds)]
    c_ref, w_ref, d_ref, og_ref, _, o_ref, out_ref, sems = refs[len(kinds) :]
    rows, width = c_ref.shape
    tile = width // tiles
    spread = spreading(rows, og_ref.shape[0])
    copies = []
    for n in range(tiles):
        columns = slice(n * tile, n * tile + tile)
        total = c_ref[:, columns] + back_sum(stride, grads, kinds, w_ref, columns)
        out_ref[:, columns] = (
            dot_nn(spread, og_ref[:, columns]) + total * d_ref[:, columns]
        ).astype(BF16)
        copy = pltpu.make_async_copy(out_ref.at[:, columns], o_ref.at[:, columns], sems.at[n])
        copy.start()
        copies.append(copy)
    for copy in copies:
        copy.wait()


def final(total, terms, taps, slope, binned, stride, after):
    kinds = [(kind, n) for kind, n, _ in terms]
    grads = [g for _, _, g in terms]
    rows, width = slope.shape
    tiles = 3
    operands = [*grads, total, taps, slope, binned, *after]
    return pl.pallas_call(
        functools.partial(final_body, stride, kinds, tiles),
        name="final",
        in_specs=[pl.BlockSpec(memory_space=pltpu.VMEM)] * len(operands),
        out_specs=pl.BlockSpec(memory_space=pltpu.HBM),
        out_shape=pltpu.HBM((rows, width), BF16),
        scratch_shapes=[pltpu.VMEM((rows, width), BF16), pltpu.SemaphoreType.DMA((tiles,))],
        compiler_params=pltpu.CompilerParams(vmem_limit_bytes=LIMIT),
        cost_estimate=cost_of(
            2 * rows * width * sum(g.shape[1] for g in grads), 8 * rows * width, 0
        ),
    )(*[pltpu.with_memory_space_constraint(v, pltpu.VMEM) for v in operands])


def local(
    seqs_in,
    pooled_grad,
    scale_in,
    shift_in,
    tap_weight_stack,
    scale_mid,
    shift_mid,
    out_weight,
    out_bias,
):
    batch, rows, width = seqs_in.shape
    count = lax.axis_size(AXIS)
    stride = DILATION_STEP // rows
    blocks = count // stride

    def hop(value, steps):
        return lax.ppermute(
            value, AXIS, [(i, i + steps) for i in range(count) if 0 <= i + steps < count]
        )

    def block_permute(value, move):
        pairs = []
        for b in range(blocks):
            to = move(b)
            if 0 <= to < blocks:
                pairs += [(b * stride + i, to * stride + i) for i in range(stride)]
        return lax.ppermute(value, AXIS, pairs)

    def swap(value):
        return block_permute(value, lambda b: b ^ 1)

    def inward(value):
        return block_permute(value, lambda b: b + 2 if b % 2 else b - 2)

    def outward(value):
        return block_permute(value, lambda b: b - 2 if b % 2 else b + 2)

    flat = seqs_in.reshape(batch * rows, width)
    binned = pooled_grad.reshape(-1, width)
    x, far_tap, act, sent0 = front(flat, scale_in, shift_in, tap_weight_stack, stride)
    taps = lax.optimization_barrier((tap_weight_stack, sent0))[0]
    came0 = inward(sent0)
    def later_than(value, *others):
        return lax.optimization_barrier((value, *others))[0]

    sent1 = side(act, far_tap, 1)
    came1 = inward(sent1)
    kept0, kept1, kept2 = keep(act, taps, [0, 1, 2], stride, [sent1])
    own = centre(act, taps, [kept0])
    joined0 = join(kept0, came0, [own[0]])
    mids0 = swap(joined0)
    sent2 = side(act, far_tap, 2, [joined0])
    came2 = inward(sent2)
    joined1 = join(kept1, came1, [sent2])
    mids1 = swap(joined1)
    hg = hidden_grad(binned, out_weight, [joined1])
    grad0, hid0 = middle(mids0, own[0], 0, scale_mid, shift_mid, hg[0])
    near0 = swap(grad0)
    joined2 = join(kept2, came2, [grad0])
    mids2 = swap(joined2)
    slope = slope_in(x, scale_in, shift_in, [joined2])
    grad1, hid1 = middle(mids1, own[1], 1, scale_mid, shift_mid, hg[1], [slope])
    near1 = swap(grad1)
    base = pooled_base(x, out_bias, [grad1])
    total = back(None, [("own", 0, grad0), ("own", 1, grad1)], taps, stride, [base])
    near0 = later_than(near0, total)
    far0 = outward(near0)
    total = back(total, [("near", 0, near0)], taps, stride)
    grad2, hid2 = middle(mids2, own[2], 2, scale_mid, shift_mid, hg[2], [total])
    before2 = hop(grad2, stride)
    later2 = hop(grad2, -stride)
    near1 = later_than(near1, grad2)
    far1 = outward(near1)
    pooled = pooled_out(base, [hid0, hid1, hid2], out_weight, batch)
    total = back(
        total, [("own", 2, grad2), ("near", 1, near1), ("far", 0, far0)], taps, stride, [hid2]
    )
    arrived = touch(later2, before2)
    out = final(
        total,
        [("later", 2, later2), ("before", 2, before2), ("far", 1, far1)],
        taps,
        slope,
        binned,
        stride,
        [arrived],
    )
    return pooled, out.reshape(seqs_in.shape)


def solution(mesh):
    in_specs = (
        P("groups", "seq", None),
        P("groups", "seq", None),
        P(),
        P(),
        P(),
        P(),
        P(),
        P(),
        P(),
    )
    out_specs = (P("groups", "seq", None), P("groups", "seq", None))
    return jax.shard_map(local, mesh=mesh, in_specs=in_specs, out_specs=out_specs, check_vma=False)
```

```python
import functools

import jax
import jax.numpy as jnp
from jax import lax
from jax.experimental import pallas as pl
from jax.experimental.pallas import tpu as pltpu
from jax.sharding import PartitionSpec as P

DILATION_STEP = 512
BIN = 4
LANES = 128
AXIS = "seq"
GELU_COEF = 0.7978845608028654
F32 = jnp.float32
BF16 = jnp.bfloat16
SHARE = 64
TILES = 6
LIMIT = 12 * 1024 * 1024


def gelu_value(v):
    inner = jnp.tanh(v * (GELU_COEF + (GELU_COEF * 0.044715) * v * v))
    half = 0.5 * v
    return half + half * inner


def gelu_both(v):
    square = v * v
    inner = jnp.tanh(v * (GELU_COEF + (GELU_COEF * 0.044715) * square))
    half = 0.5 * v
    value = half + half * inner
    slope = (0.5 + 0.5 * inner) + half * (1.0 - inner * inner) * (
        GELU_COEF + (GELU_COEF * 0.134145) * square
    )
    return value, slope


def gelu_slope(v):
    return gelu_both(v)[1]


def dot_nn(a, b):
    return jnp.dot(a, b, preferred_element_type=F32)


def dot_nt(a, b):
    return lax.dot_general(a, b, (((1,), (1,)), ((), ())), preferred_element_type=F32)


def averaging(bins, rows):
    row = lax.broadcasted_iota(jnp.int32, (bins, rows), 0)
    column = lax.broadcasted_iota(jnp.int32, (bins, rows), 1)
    inside = (column >= row * BIN) & (column < row * BIN + BIN)
    return jnp.where(inside, 1.0 / BIN, 0.0).astype(BF16)


def spreading(rows, bins):
    row = lax.broadcasted_iota(jnp.int32, (rows, bins), 0)
    column = lax.broadcasted_iota(jnp.int32, (rows, bins), 1)
    inside = (row >= column * BIN) & (row < column * BIN + BIN)
    return jnp.where(inside, 1.0 / BIN, 0.0).astype(BF16)


def near_tap(stride):
    return 2 * lax.rem(lax.div(lax.axis_index(AXIS), stride), 2)


def cost_of(flops, nbytes, trans):
    return pl.CostEstimate(
        flops=flops // SHARE, bytes_accessed=nbytes // SHARE, transcendentals=trans // SHARE
    )


def local_call(body, name, operands, outs, cost, scratch=(), after=()):
    flops, nbytes, trans = cost
    single = not isinstance(outs, list)
    space = pl.BlockSpec(memory_space=pltpu.VMEM)
    if after:
        inner, skip = body, len(operands)
        body = lambda *refs: inner(*refs[:skip], *refs[skip + len(after) :])
        operands = [*operands, *after]
    shapes = [pltpu.VMEM(s, d) for s, d in ([outs] if single else outs)]
    return pl.pallas_call(
        body,
        name=name,
        in_specs=[space] * len(operands),
        out_specs=space if single else [space] * len(outs),
        out_shape=shapes[0] if single else shapes,
        scratch_shapes=list(scratch),
        compiler_params=pltpu.CompilerParams(vmem_limit_bytes=LIMIT),
        cost_estimate=cost_of(flops, nbytes, trans),
    )(*[pltpu.with_memory_space_constraint(v, pltpu.VMEM) for v in operands])

SPLITS = (256, 256, 256)


def bounds(n):
    return slice(sum(SPLITS[:n]), sum(SPLITS[: n + 1]))


def front_body(stride, x_hbm, s_hbm, b_hbm, w_hbm, x_ref, w_ref, a_ref, p_ref, s_ref, b_ref, sems):
    rows, width = x_ref.shape
    slabs = 4
    slab = rows // slabs
    copies = [
        pltpu.make_async_copy(s_hbm, s_ref, sems.at[0]),
        pltpu.make_async_copy(b_hbm, b_ref, sems.at[1]),
    ]
    copies += [
        pltpu.make_async_copy(
            x_hbm.at[pl.ds(n * slab, slab)], x_ref.at[pl.ds(n * slab, slab)], sems.at[2 + n]
        )
        for n in range(slabs)
    ]
    taps = pltpu.make_async_copy(w_hbm.at[2 - near_tap(stride)], w_ref, sems.at[2 + slabs])
    for copy in copies:
        copy.start()
    taps.start()
    copies[0].wait()
    copies[1].wait()
    scale = s_ref[...].reshape(1, width)
    shift = b_ref[...].reshape(1, width)
    for n, copy in enumerate(copies[2:]):
        copy.wait()
        part = slice(n * slab, n * slab + slab)
        a_ref[part, :] = gelu_value(x_ref[part, :].astype(F32) * scale + shift).astype(BF16)
    taps.wait()
    p_ref[...] = dot_nn(a_ref[...], w_ref[:, bounds(0)]).astype(BF16)


def front(x, scale, shift, taps, stride):
    rows, width = x.shape
    mid = SPLITS[0]
    space = pl.BlockSpec(memory_space=pltpu.VMEM)
    far = pl.BlockSpec(memory_space=pltpu.HBM)
    operands = [pltpu.with_memory_space_constraint(v, pltpu.HBM) for v in (x, scale, shift, taps)]
    return pl.pallas_call(
        functools.partial(front_body, stride),
        name="front",
        in_specs=[far] * 4,
        out_specs=[space] * 4,
        out_shape=[
            pltpu.VMEM(x.shape, BF16),
            pltpu.VMEM(taps.shape[1:], BF16),
            pltpu.VMEM((rows, width), BF16),
            pltpu.VMEM((rows, mid), BF16),
        ],
        scratch_shapes=[
            pltpu.VMEM((width,), F32),
            pltpu.VMEM((width,), F32),
            pltpu.SemaphoreType.DMA((7,)),
        ],
        compiler_params=pltpu.CompilerParams(vmem_limit_bytes=LIMIT),
        cost_estimate=cost_of(2 * rows * width * mid, 2 * (x.size + taps.size), x.size),
    )(*operands)


def side_body(which, a_ref, w_ref, o_ref):
    o_ref[...] = dot_nn(a_ref[...], w_ref[:, bounds(which)]).astype(BF16)


def side(act, far_tap, which, after=()):
    rows, width = act.shape
    return local_call(
        functools.partial(side_body, which),
        "side",
        [act, far_tap],
        ((rows, SPLITS[which]), BF16),
        (2 * rows * width * SPLITS[which], 2 * rows * width, 0),
        after=after,
    )


def keep_body(stride, which, a_ref, w_ref, *outs):
    for n, out in zip(which, outs):
        out[...] = dot_nn(a_ref[...], w_ref[near_tap(stride), :, bounds(n)])


def keep(act, taps, which, stride, after=()):
    rows, width = act.shape
    return local_call(
        functools.partial(keep_body, stride, which),
        "keep",
        [act, taps],
        [((rows, SPLITS[n]), F32) for n in which],
        (2 * rows * width * sum(SPLITS[n] for n in which), 2 * rows * width, 0),
        after=after,
    )


def centre_body(a_ref, w_ref, *outs):
    for n, out in enumerate(outs):
        out[...] = dot_nn(a_ref[...], w_ref[1, :, bounds(n)])


def centre(act, taps, after):
    rows, width = act.shape
    return local_call(
        centre_body,
        "centre",
        [act, taps],
        [((rows, c), F32) for c in SPLITS],
        (2 * rows * width * sum(SPLITS), 2 * rows * width, 0),
        after=after,
    )


def join_body(k_ref, r_ref, o_ref):
    o_ref[...] = (k_ref[...] + r_ref[...].astype(F32)).astype(BF16)


def join(kept, came, after=()):
    return local_call(
        join_body,
        "join",
        [kept, came],
        (kept.shape, BF16),
        (kept.size, 8 * kept.size, 0),
        after=after,
    )


def hidden_grad_body(g_ref, w_ref, *outs):
    grad = (g_ref[...].astype(F32) * (1.0 / BIN)).astype(BF16)
    for n, out in enumerate(outs):
        out[...] = dot_nt(grad, w_ref[bounds(n), :])


def hidden_grad(binned, weight, after):
    bins, width = binned.shape
    mid = weight.shape[0]
    return local_call(
        hidden_grad_body,
        "hidden_grad",
        [binned, weight],
        [((bins, c), F32) for c in SPLITS],
        (2 * bins * width * mid, 2 * bins * width, 0),
        after=after,
    )


def middle_body(which, t_ref, p_ref, s_ref, b_ref, hg_ref, g_ref, h_ref, wide_ref):
    bins, width = hg_ref.shape
    for lane in range(width // LANES):
        columns = slice(lane * LANES, lane * LANES + LANES)
        for k in range(BIN):
            wide_ref[lane, pl.ds(k, bins, stride=BIN), :] = hg_ref[:, columns]
    first = bounds(which).start
    scales = s_ref[...].reshape(1, s_ref.shape[0])
    shifts = b_ref[...].reshape(1, b_ref.shape[0])
    for lane in range(width // LANES):
        columns = slice(lane * LANES, lane * LANES + LANES)
        among = slice(first + lane * LANES, first + lane * LANES + LANES)
        mid = p_ref[:, columns] + t_ref[:, columns].astype(F32)
        scale = scales[:, among]
        value, slope = gelu_both(mid * scale + shifts[:, among])
        g_ref[:, columns] = (wide_ref[lane] * slope * scale).astype(BF16)
        h_ref[:, columns] = value.astype(BF16)


def middle(part, centre_part, which, scale, shift, hidden_grads, after=()):
    rows, mid = centre_part.shape
    return local_call(
        functools.partial(middle_body, which),
        "middle",
        [part, centre_part, scale, shift, hidden_grads],
        [((rows, mid), BF16), ((rows, mid), BF16)],
        (30 * rows * mid, 12 * rows * mid, rows * mid),
        scratch=[pltpu.VMEM((mid // LANES, rows, LANES), F32)],
        after=after,
    )


def pooled_base_body(x_ref, b_ref, o_ref):
    bins, width = o_ref.shape
    average = averaging(bins, x_ref.shape[0])
    o_ref[...] = dot_nn(average, x_ref[...]) + b_ref[...].reshape(1, width)


def pooled_base(x, bias, after):
    rows, width = x.shape
    bins = rows // BIN
    return local_call(
        pooled_base_body,
        "pooled_base",
        [x, bias],
        ((bins, width), F32),
        (2 * bins * width * rows, 2 * rows * width, 0),
        after=after,
    )


def pooled_body(*refs):
    count = len(SPLITS)
    hidden = refs[:count]
    base_ref, w_ref, o_ref, mark_ref, out_ref, sem = refs[count:]
    bins, width = out_ref.shape
    rows = hidden[0].shape[0]
    average = averaging(bins, rows)
    total = base_ref[...]
    for n in range(count):
        mean = dot_nn(average, hidden[n][...]).astype(BF16)
        total = total + dot_nn(mean, w_ref[bounds(n), :])
    out_ref[...] = total.astype(BF16)
    mark_ref[...] = out_ref[:16, :LANES]
    half = bins // o_ref.shape[0]
    for n in range(o_ref.shape[0]):
        copy = pltpu.make_async_copy(out_ref.at[pl.ds(n * half, half)], o_ref.at[n], sem.at[n])
        copy.start()
    for n in range(o_ref.shape[0]):
        copy = pltpu.make_async_copy(out_ref.at[pl.ds(n * half, half)], o_ref.at[n], sem.at[n])
        copy.wait()


def pooled_out(base, hidden, weight, batch):
    bins, width = base.shape
    mid = weight.shape[0]
    operands = [*hidden, base, weight]
    return pl.pallas_call(
        pooled_body,
        name="pooled",
        in_specs=[pl.BlockSpec(memory_space=pltpu.VMEM)] * len(operands),
        out_specs=[pl.BlockSpec(memory_space=pltpu.HBM), pl.BlockSpec(memory_space=pltpu.VMEM)],
        out_shape=[
            pltpu.HBM((batch, bins // batch, width), BF16),
            pltpu.VMEM((16, LANES), BF16),
        ],
        scratch_shapes=[pltpu.VMEM((bins, width), BF16), pltpu.SemaphoreType.DMA((batch,))],
        compiler_params=pltpu.CompilerParams(vmem_limit_bytes=LIMIT),
        cost_estimate=cost_of(2 * bins * width * mid, 6 * bins * width, 0),
    )(*[pltpu.with_memory_space_constraint(v, pltpu.VMEM) for v in operands])


def slope_body(x_ref, s_ref, b_ref, o_ref):
    width = x_ref.shape[1]
    scale = s_ref[...].reshape(1, width)
    shift = b_ref[...].reshape(1, width)
    o_ref[...] = gelu_slope(x_ref[...].astype(F32) * scale + shift) * scale


def slope_in(x, scale, shift, after):
    return local_call(
        slope_body,
        "slope",
        [x, scale, shift],
        (x.shape, F32),
        (30 * x.size, 6 * x.size, x.size),
        after=after,
    )


def back_sum(stride, refs, kinds, w_ref, columns=slice(None)):
    near = near_tap(stride)
    taps = dict(own=1, near=near, far=2 - near, before=2, later=0)
    total = None
    for ref, (kind, n) in zip(refs, kinds):
        term = dot_nt(ref[...], w_ref[taps[kind], columns, bounds(n)])
        total = term if total is None else total + term
    return total


def back_body(stride, kinds, started, *refs):
    grads = refs[: len(kinds)]
    rest = refs[len(kinds) :]
    w_ref, o_ref = rest[0], rest[-1]
    total = back_sum(stride, grads, kinds, w_ref)
    o_ref[...] = rest[1][...] + total if started else total


def back(total, terms, taps, stride, after=()):
    kinds = [(kind, n) for kind, n, _ in terms]
    grads = [g for _, _, g in terms]
    rows = grads[0].shape[0]
    width = taps.shape[1]
    started = total is not None
    return local_call(
        functools.partial(back_body, stride, kinds, started),
        "back",
        [*grads, taps] + ([total] if started else []),
        ((rows, width), F32),
        (2 * rows * width * sum(g.shape[1] for g in grads), 8 * rows * width, 0),
        after=after,
    )


def touch_body(a_ref, b_ref, o_ref):
    o_ref[...] = a_ref[:16, :LANES] + b_ref[:16, :LANES]


def touch(a, b, after):
    return local_call(touch_body, "touch", [a, b], ((16, LANES), BF16), (1, 1, 0), after=after)


def settle_body(stride, kinds, *refs):
    grads = refs[: len(kinds)]
    c_ref, w_ref, d_ref, og_ref, o_ref = refs[len(kinds) :]
    spread = spreading(c_ref.shape[0], og_ref.shape[0])
    total = c_ref[...] + back_sum(stride, grads, kinds, w_ref)
    o_ref[...] = dot_nn(spread, og_ref[...]) + total * d_ref[...]


def settle(total, terms, taps, slope, binned, stride):
    kinds = [(kind, n) for kind, n, _ in terms]
    grads = [g for _, _, g in terms]
    rows, width = slope.shape
    return local_call(
        functools.partial(settle_body, stride, kinds),
        "settle",
        [*grads, total, taps, slope, binned],
        ((rows, width), F32),
        (2 * rows * width * sum(g.shape[1] for g in grads), 8 * rows * width, 0),
    )


def final_body(stride, kinds, tiles, *refs):
    grads = refs[: len(kinds)]
    c_ref, w_ref, d_ref, o_ref, out_ref, sems = refs[len(kinds) :]
    rows, width = c_ref.shape
    tile = width // tiles
    copies = []
    for n in range(tiles):
        columns = slice(n * tile, n * tile + tile)
        last = back_sum(stride, grads, kinds, w_ref, columns)
        out_ref[:, columns] = (c_ref[:, columns] + last * d_ref[:, columns]).astype(BF16)
        copy = pltpu.make_async_copy(out_ref.at[:, columns], o_ref.at[:, columns], sems.at[n])
        copy.start()
        copies.append(copy)
    for copy in copies:
        copy.wait()


def final(settled, terms, taps, slope, stride):
    kinds = [(kind, n) for kind, n, _ in terms]
    grads = [g for _, _, g in terms]
    rows, width = slope.shape
    tiles = TILES
    operands = [*grads, settled, taps, slope]
    return pl.pallas_call(
        functools.partial(final_body, stride, kinds, tiles),
        name="final",
        in_specs=[pl.BlockSpec(memory_space=pltpu.VMEM)] * len(operands),
        out_specs=pl.BlockSpec(memory_space=pltpu.HBM),
        out_shape=pltpu.HBM((rows, width), BF16),
        scratch_shapes=[pltpu.VMEM((rows, width), BF16), pltpu.SemaphoreType.DMA((tiles,))],
        compiler_params=pltpu.CompilerParams(vmem_limit_bytes=LIMIT),
        cost_estimate=cost_of(
            2 * rows * width * sum(g.shape[1] for g in grads), 8 * rows * width, 0
        ),
    )(*[pltpu.with_memory_space_constraint(v, pltpu.VMEM) for v in operands])


def local(
    seqs_in,
    pooled_grad,
    scale_in,
    shift_in,
    tap_weight_stack,
    scale_mid,
    shift_mid,
    out_weight,
    out_bias,
):
    batch, rows, width = seqs_in.shape
    count = lax.axis_size(AXIS)
    stride = DILATION_STEP // rows
    blocks = count // stride

    def hop(value, steps):
        return lax.ppermute(
            value, AXIS, [(i, i + steps) for i in range(count) if 0 <= i + steps < count]
        )

    def block_permute(value, move):
        pairs = []
        for b in range(blocks):
            to = move(b)
            if 0 <= to < blocks:
                pairs += [(b * stride + i, to * stride + i) for i in range(stride)]
        return lax.ppermute(value, AXIS, pairs)

    def swap(value):
        return block_permute(value, lambda b: b ^ 1)

    def inward(value):
        return block_permute(value, lambda b: b + 2 if b % 2 else b - 2)

    def outward(value):
        return block_permute(value, lambda b: b - 2 if b % 2 else b + 2)

    flat = seqs_in.reshape(batch * rows, width)
    binned = pooled_grad.reshape(-1, width)
    x, far_tap, act, sent0 = front(flat, scale_in, shift_in, tap_weight_stack, stride)
    taps = lax.optimization_barrier((tap_weight_stack, sent0))[0]
    came0 = inward(sent0)
    def later_than(value, *others):
        return lax.optimization_barrier((value, *others))[0]

    kept0, kept1, kept2 = keep(act, taps, [0, 1, 2], stride)
    own = centre(act, taps, [kept0])
    sent1 = side(act, far_tap, 1, [own[0]])
    came1 = inward(sent1)
    joined0 = join(kept0, came0, [sent1])
    mids0 = swap(joined0)
    sent2 = side(act, far_tap, 2, [joined0])
    came2 = inward(sent2)
    joined1 = join(kept1, came1, [sent2])
    mids1 = swap(joined1)
    hg = hidden_grad(binned, out_weight, [joined1])
    grad0, hid0 = middle(mids0, own[0], 0, scale_mid, shift_mid, hg[0])
    near0 = swap(grad0)
    joined2 = join(kept2, came2, [grad0])
    mids2 = swap(joined2)
    slope = slope_in(x, scale_in, shift_in, [joined2])
    grad1, hid1 = middle(mids1, own[1], 1, scale_mid, shift_mid, hg[1], [slope])
    near1 = swap(grad1)
    base = pooled_base(x, out_bias, [grad1])
    total = back(None, [("own", 0, grad0), ("own", 1, grad1)], taps, stride, [base])
    near0 = later_than(near0, total)
    far0 = outward(near0)
    total = back(total, [("near", 0, near0)], taps, stride)
    grad2, hid2 = middle(mids2, own[2], 2, scale_mid, shift_mid, hg[2], [total])
    near2 = swap(grad2)
    pooled, mean2 = pooled_out(base, [hid0, hid1, hid2], out_weight, batch)
    near1, mean2 = lax.optimization_barrier((near1, mean2))
    far1 = outward(near1)
    mark = touch(far0, near1, [mean2])
    near2, mark = lax.optimization_barrier((near2, mark))
    far2 = outward(near2)
    total = back(
        total,
        [("own", 2, grad2), ("far", 0, far0), ("near", 1, near1), ("near", 2, near2)],
        taps,
        stride,
        [mark],
    )
    settled = settle(total, [("far", 1, far1)], taps, slope, binned, stride)
    out = final(settled, [("far", 2, far2)], taps, slope, stride)
    return pooled, out.reshape(seqs_in.shape)


def solution(mesh):
    in_specs = (
        P("groups", "seq", None),
        P("groups", "seq", None),
        P(),
        P(),
        P(),
        P(),
        P(),
        P(),
        P(),
    )
    out_specs = (P("groups", "seq", None), P("groups", "seq", None))
    return jax.shard_map(local, mesh=mesh, in_specs=in_specs, out_specs=out_specs, check_vma=False)
```

```python
import functools

import jax
import jax.numpy as jnp
from jax import lax
from jax.experimental import pallas as pl
from jax.experimental.pallas import tpu as pltpu
from jax.sharding import PartitionSpec as P

DILATION_STEP = 512
BIN = 4
LANES = 128
AXIS = "seq"
GELU_COEF = 0.7978845608028654
F32 = jnp.float32
BF16 = jnp.bfloat16
SHARE = 64
TILES = 6
LIMIT = 12 * 1024 * 1024


def gelu_value(v):
    inner = jnp.tanh(v * (GELU_COEF + (GELU_COEF * 0.044715) * v * v))
    half = 0.5 * v
    return half + half * inner


def gelu_both(v):
    square = v * v
    inner = jnp.tanh(v * (GELU_COEF + (GELU_COEF * 0.044715) * square))
    half = 0.5 * v
    value = half + half * inner
    slope = (0.5 + 0.5 * inner) + half * (1.0 - inner * inner) * (
        GELU_COEF + (GELU_COEF * 0.134145) * square
    )
    return value, slope


def gelu_slope(v):
    return gelu_both(v)[1]


def dot_nn(a, b):
    return jnp.dot(a, b, preferred_element_type=F32)


def dot_nt(a, b):
    return lax.dot_general(a, b, (((1,), (1,)), ((), ())), preferred_element_type=F32)


def averaging(bins, rows):
    row = lax.broadcasted_iota(jnp.int32, (bins, rows), 0)
    column = lax.broadcasted_iota(jnp.int32, (bins, rows), 1)
    inside = (column >= row * BIN) & (column < row * BIN + BIN)
    return jnp.where(inside, 1.0 / BIN, 0.0).astype(BF16)


def spreading(rows, bins):
    row = lax.broadcasted_iota(jnp.int32, (rows, bins), 0)
    column = lax.broadcasted_iota(jnp.int32, (rows, bins), 1)
    inside = (row >= column * BIN) & (row < column * BIN + BIN)
    return jnp.where(inside, 1.0 / BIN, 0.0).astype(BF16)


def near_tap(stride):
    return 2 * lax.rem(lax.div(lax.axis_index(AXIS), stride), 2)


def cost_of(flops, nbytes, trans):
    return pl.CostEstimate(
        flops=flops // SHARE, bytes_accessed=nbytes // SHARE, transcendentals=trans // SHARE
    )


def local_call(body, name, operands, outs, cost, scratch=(), after=()):
    flops, nbytes, trans = cost
    single = not isinstance(outs, list)
    space = pl.BlockSpec(memory_space=pltpu.VMEM)
    if after:
        inner, skip = body, len(operands)
        body = lambda *refs: inner(*refs[:skip], *refs[skip + len(after) :])
        operands = [*operands, *after]
    shapes = [pltpu.VMEM(s, d) for s, d in ([outs] if single else outs)]
    return pl.pallas_call(
        body,
        name=name,
        in_specs=[space] * len(operands),
        out_specs=space if single else [space] * len(outs),
        out_shape=shapes[0] if single else shapes,
        scratch_shapes=list(scratch),
        compiler_params=pltpu.CompilerParams(vmem_limit_bytes=LIMIT),
        cost_estimate=cost_of(flops, nbytes, trans),
    )(*[pltpu.with_memory_space_constraint(v, pltpu.VMEM) for v in operands])

SPLITS = (256, 256, 256)


def bounds(n):
    return slice(sum(SPLITS[:n]), sum(SPLITS[: n + 1]))


def front_body(stride, x_hbm, s_hbm, b_hbm, w_hbm, x_ref, w_ref, a_ref, p_ref, s_ref, b_ref, sems):
    rows, width = x_ref.shape
    slabs = 4
    slab = rows // slabs
    copies = [
        pltpu.make_async_copy(s_hbm, s_ref, sems.at[0]),
        pltpu.make_async_copy(b_hbm, b_ref, sems.at[1]),
    ]
    copies += [
        pltpu.make_async_copy(
            x_hbm.at[pl.ds(n * slab, slab)], x_ref.at[pl.ds(n * slab, slab)], sems.at[2 + n]
        )
        for n in range(slabs)
    ]
    taps = pltpu.make_async_copy(w_hbm.at[2 - near_tap(stride)], w_ref, sems.at[2 + slabs])
    for copy in copies:
        copy.start()
    taps.start()
    copies[0].wait()
    copies[1].wait()
    scale = s_ref[...].reshape(1, width)
    shift = b_ref[...].reshape(1, width)
    for n, copy in enumerate(copies[2:]):
        copy.wait()
        part = slice(n * slab, n * slab + slab)
        a_ref[part, :] = gelu_value(x_ref[part, :].astype(F32) * scale + shift).astype(BF16)
    taps.wait()
    p_ref[...] = dot_nn(a_ref[...], w_ref[:, bounds(0)]).astype(BF16)


def front(x, scale, shift, taps, stride):
    rows, width = x.shape
    mid = SPLITS[0]
    space = pl.BlockSpec(memory_space=pltpu.VMEM)
    far = pl.BlockSpec(memory_space=pltpu.HBM)
    operands = [pltpu.with_memory_space_constraint(v, pltpu.HBM) for v in (x, scale, shift, taps)]
    return pl.pallas_call(
        functools.partial(front_body, stride),
        name="front",
        in_specs=[far] * 4,
        out_specs=[space] * 4,
        out_shape=[
            pltpu.VMEM(x.shape, BF16),
            pltpu.VMEM(taps.shape[1:], BF16),
            pltpu.VMEM((rows, width), BF16),
            pltpu.VMEM((rows, mid), BF16),
        ],
        scratch_shapes=[
            pltpu.VMEM((width,), F32),
            pltpu.VMEM((width,), F32),
            pltpu.SemaphoreType.DMA((7,)),
        ],
        compiler_params=pltpu.CompilerParams(vmem_limit_bytes=LIMIT),
        cost_estimate=cost_of(2 * rows * width * mid, 2 * (x.size + taps.size), x.size),
    )(*operands)


def side_body(which, a_ref, w_ref, o_ref):
    o_ref[...] = dot_nn(a_ref[...], w_ref[:, bounds(which)]).astype(BF16)


def side(act, far_tap, which, after=()):
    rows, width = act.shape
    return local_call(
        functools.partial(side_body, which),
        "side",
        [act, far_tap],
        ((rows, SPLITS[which]), BF16),
        (2 * rows * width * SPLITS[which], 2 * rows * width, 0),
        after=after,
    )


def near_side_body(which, stride, a_ref, w_ref, o_ref):
    o_ref[...] = dot_nn(a_ref[...], w_ref[near_tap(stride), :, bounds(which)]).astype(BF16)


def near_side(act, taps, which, stride):
    rows, width = act.shape
    return local_call(
        functools.partial(near_side_body, which, stride),
        "near_side",
        [act, taps],
        ((rows, SPLITS[which]), BF16),
        (2 * rows * width * SPLITS[which], 2 * rows * width, 0),
    )


def keep_body(stride, which, a_ref, w_ref, *outs):
    for n, out in zip(which, outs):
        out[...] = dot_nn(a_ref[...], w_ref[near_tap(stride), :, bounds(n)])


def keep(act, taps, which, stride, after=()):
    rows, width = act.shape
    return local_call(
        functools.partial(keep_body, stride, which),
        "keep",
        [act, taps],
        [((rows, SPLITS[n]), F32) for n in which],
        (2 * rows * width * sum(SPLITS[n] for n in which), 2 * rows * width, 0),
        after=after,
    )


def centre_body(which, a_ref, w_ref, *outs):
    for n, out in zip(which, outs):
        out[...] = dot_nn(a_ref[...], w_ref[1, :, bounds(n)])


def centre(act, taps, which, after):
    rows, width = act.shape
    return local_call(
        functools.partial(centre_body, which),
        "centre",
        [act, taps],
        [((rows, SPLITS[n]), F32) for n in which],
        (2 * rows * width * sum(SPLITS[n] for n in which), 2 * rows * width, 0),
        after=after,
    )


def join_body(k_ref, r_ref, o_ref):
    o_ref[...] = (k_ref[...] + r_ref[...].astype(F32)).astype(BF16)


def join(kept, came, after=()):
    return local_call(
        join_body,
        "join",
        [kept, came],
        (kept.shape, BF16),
        (kept.size, 8 * kept.size, 0),
        after=after,
    )


def hidden_grad_body(g_ref, w_ref, *outs):
    grad = (g_ref[...].astype(F32) * (1.0 / BIN)).astype(BF16)
    for n, out in enumerate(outs):
        out[...] = dot_nt(grad, w_ref[bounds(n), :])


def hidden_grad(binned, weight, after):
    bins, width = binned.shape
    mid = weight.shape[0]
    return local_call(
        hidden_grad_body,
        "hidden_grad",
        [binned, weight],
        [((bins, c), F32) for c in SPLITS],
        (2 * bins * width * mid, 2 * bins * width, 0),
        after=after,
    )


def middle_body(count, which, *refs):
    parts = refs[:count]
    p_ref, s_ref, b_ref, hg_ref, g_ref, h_ref, wide_ref = refs[count:]
    bins, width = hg_ref.shape
    for lane in range(width // LANES):
        columns = slice(lane * LANES, lane * LANES + LANES)
        for k in range(BIN):
            wide_ref[lane, pl.ds(k, bins, stride=BIN), :] = hg_ref[:, columns]
    first = bounds(which).start
    scales = s_ref[...].reshape(1, s_ref.shape[0])
    shifts = b_ref[...].reshape(1, b_ref.shape[0])
    for lane in range(width // LANES):
        columns = slice(lane * LANES, lane * LANES + LANES)
        among = slice(first + lane * LANES, first + lane * LANES + LANES)
        mid = p_ref[:, columns]
        for part in parts:
            mid = mid + part[:, columns].astype(F32)
        scale = scales[:, among]
        value, slope = gelu_both(mid * scale + shifts[:, among])
        g_ref[:, columns] = (wide_ref[lane] * slope * scale).astype(BF16)
        h_ref[:, columns] = value.astype(BF16)


def middle(parts, centre_part, which, scale, shift, hidden_grads, after=()):
    rows, mid = centre_part.shape
    return local_call(
        functools.partial(middle_body, len(parts), which),
        "middle",
        [*parts, centre_part, scale, shift, hidden_grads],
        [((rows, mid), BF16), ((rows, mid), BF16)],
        (30 * rows * mid, 12 * rows * mid, rows * mid),
        scratch=[pltpu.VMEM((mid // LANES, rows, LANES), F32)],
        after=after,
    )


def pooled_base_body(x_ref, b_ref, o_ref):
    bins, width = o_ref.shape
    average = averaging(bins, x_ref.shape[0])
    o_ref[...] = dot_nn(average, x_ref[...]) + b_ref[...].reshape(1, width)


def pooled_base(x, bias, after):
    rows, width = x.shape
    bins = rows // BIN
    return local_call(
        pooled_base_body,
        "pooled_base",
        [x, bias],
        ((bins, width), F32),
        (2 * bins * width * rows, 2 * rows * width, 0),
        after=after,
    )


def pooled_body(*refs):
    count = len(SPLITS)
    hidden = refs[:count]
    base_ref, w_ref, o_ref, mark_ref, out_ref, sem = refs[count:]
    bins, width = out_ref.shape
    rows = hidden[0].shape[0]
    average = averaging(bins, rows)
    total = base_ref[...]
    for n in range(count):
        mean = dot_nn(average, hidden[n][...]).astype(BF16)
        total = total + dot_nn(mean, w_ref[bounds(n), :])
    out_ref[...] = total.astype(BF16)
    mark_ref[...] = out_ref[:16, :LANES]
    half = bins // o_ref.shape[0]
    for n in range(o_ref.shape[0]):
        copy = pltpu.make_async_copy(out_ref.at[pl.ds(n * half, half)], o_ref.at[n], sem.at[n])
        copy.start()
    for n in range(o_ref.shape[0]):
        copy = pltpu.make_async_copy(out_ref.at[pl.ds(n * half, half)], o_ref.at[n], sem.at[n])
        copy.wait()


def pooled_out(base, hidden, weight, batch):
    bins, width = base.shape
    mid = weight.shape[0]
    operands = [*hidden, base, weight]
    return pl.pallas_call(
        pooled_body,
        name="pooled",
        in_specs=[pl.BlockSpec(memory_space=pltpu.VMEM)] * len(operands),
        out_specs=[pl.BlockSpec(memory_space=pltpu.HBM), pl.BlockSpec(memory_space=pltpu.VMEM)],
        out_shape=[
            pltpu.HBM((batch, bins // batch, width), BF16),
            pltpu.VMEM((16, LANES), BF16),
        ],
        scratch_shapes=[pltpu.VMEM((bins, width), BF16), pltpu.SemaphoreType.DMA((batch,))],
        compiler_params=pltpu.CompilerParams(vmem_limit_bytes=LIMIT),
        cost_estimate=cost_of(2 * bins * width * mid, 6 * bins * width, 0),
    )(*[pltpu.with_memory_space_constraint(v, pltpu.VMEM) for v in operands])


def slope_body(x_ref, s_ref, b_ref, o_ref):
    width = x_ref.shape[1]
    scale = s_ref[...].reshape(1, width)
    shift = b_ref[...].reshape(1, width)
    o_ref[...] = gelu_slope(x_ref[...].astype(F32) * scale + shift) * scale


def slope_in(x, scale, shift, after):
    return local_call(
        slope_body,
        "slope",
        [x, scale, shift],
        (x.shape, F32),
        (30 * x.size, 6 * x.size, x.size),
        after=after,
    )


def back_sum(stride, refs, kinds, w_ref, columns=slice(None)):
    near = near_tap(stride)
    taps = dict(own=1, near=near, far=2 - near, before=2, later=0)
    total = None
    for ref, (kind, n) in zip(refs, kinds):
        term = dot_nt(ref[...], w_ref[taps[kind], columns, bounds(n)])
        total = term if total is None else total + term
    return total


def back_body(stride, kinds, started, *refs):
    grads = refs[: len(kinds)]
    rest = refs[len(kinds) :]
    w_ref, o_ref = rest[0], rest[-1]
    total = back_sum(stride, grads, kinds, w_ref)
    o_ref[...] = rest[1][...] + total if started else total


def back(total, terms, taps, stride, after=()):
    kinds = [(kind, n) for kind, n, _ in terms]
    grads = [g for _, _, g in terms]
    rows = grads[0].shape[0]
    width = taps.shape[1]
    started = total is not None
    return local_call(
        functools.partial(back_body, stride, kinds, started),
        "back",
        [*grads, taps] + ([total] if started else []),
        ((rows, width), F32),
        (2 * rows * width * sum(g.shape[1] for g in grads), 8 * rows * width, 0),
        after=after,
    )


def touch_body(a_ref, b_ref, o_ref):
    o_ref[...] = a_ref[:16, :LANES] + b_ref[:16, :LANES]


def touch(a, b, after):
    return local_call(touch_body, "touch", [a, b], ((16, LANES), BF16), (1, 1, 0), after=after)


def settle_body(stride, kinds, *refs):
    grads = refs[: len(kinds)]
    c_ref, w_ref, d_ref, og_ref, o_ref = refs[len(kinds) :]
    spread = spreading(c_ref.shape[0], og_ref.shape[0])
    total = c_ref[...] + back_sum(stride, grads, kinds, w_ref)
    o_ref[...] = dot_nn(spread, og_ref[...]) + total * d_ref[...]


def settle(total, terms, taps, slope, binned, stride):
    kinds = [(kind, n) for kind, n, _ in terms]
    grads = [g for _, _, g in terms]
    rows, width = slope.shape
    return local_call(
        functools.partial(settle_body, stride, kinds),
        "settle",
        [*grads, total, taps, slope, binned],
        ((rows, width), F32),
        (2 * rows * width * sum(g.shape[1] for g in grads), 8 * rows * width, 0),
    )


def final_body(stride, kinds, tiles, *refs):
    grads = refs[: len(kinds)]
    c_ref, w_ref, d_ref, o_ref, out_ref, sems = refs[len(kinds) :]
    rows, width = c_ref.shape
    tile = width // tiles
    copies = []
    for n in range(tiles):
        columns = slice(n * tile, n * tile + tile)
        last = back_sum(stride, grads, kinds, w_ref, columns)
        out_ref[:, columns] = (c_ref[:, columns] + last * d_ref[:, columns]).astype(BF16)
        copy = pltpu.make_async_copy(out_ref.at[:, columns], o_ref.at[:, columns], sems.at[n])
        copy.start()
        copies.append(copy)
    for copy in copies:
        copy.wait()


def final(settled, terms, taps, slope, stride):
    kinds = [(kind, n) for kind, n, _ in terms]
    grads = [g for _, _, g in terms]
    rows, width = slope.shape
    tiles = TILES
    operands = [*grads, settled, taps, slope]
    return pl.pallas_call(
        functools.partial(final_body, stride, kinds, tiles),
        name="final",
        in_specs=[pl.BlockSpec(memory_space=pltpu.VMEM)] * len(operands),
        out_specs=pl.BlockSpec(memory_space=pltpu.HBM),
        out_shape=pltpu.HBM((rows, width), BF16),
        scratch_shapes=[pltpu.VMEM((rows, width), BF16), pltpu.SemaphoreType.DMA((tiles,))],
        compiler_params=pltpu.CompilerParams(vmem_limit_bytes=LIMIT),
        cost_estimate=cost_of(
            2 * rows * width * sum(g.shape[1] for g in grads), 8 * rows * width, 0
        ),
    )(*[pltpu.with_memory_space_constraint(v, pltpu.VMEM) for v in operands])


def local(
    seqs_in,
    pooled_grad,
    scale_in,
    shift_in,
    tap_weight_stack,
    scale_mid,
    shift_mid,
    out_weight,
    out_bias,
):
    batch, rows, width = seqs_in.shape
    count = lax.axis_size(AXIS)
    stride = DILATION_STEP // rows
    blocks = count // stride

    def hop(value, steps):
        return lax.ppermute(
            value, AXIS, [(i, i + steps) for i in range(count) if 0 <= i + steps < count]
        )

    def block_permute(value, move):
        pairs = []
        for b in range(blocks):
            to = move(b)
            if 0 <= to < blocks:
                pairs += [(b * stride + i, to * stride + i) for i in range(stride)]
        return lax.ppermute(value, AXIS, pairs)

    def swap(value):
        return block_permute(value, lambda b: b ^ 1)

    def across(value):
        return block_permute(value, lambda b: b + 1 if b % 2 else b - 1)

    def inward(value):
        return block_permute(value, lambda b: b + 2 if b % 2 else b - 2)

    def outward(value):
        return block_permute(value, lambda b: b - 2 if b % 2 else b + 2)

    flat = seqs_in.reshape(batch * rows, width)
    binned = pooled_grad.reshape(-1, width)
    x, far_tap, act, sent0 = front(flat, scale_in, shift_in, tap_weight_stack, stride)
    taps = lax.optimization_barrier((tap_weight_stack, sent0))[0]
    far_part0 = across(sent0)
    near_side0 = near_side(act, taps, 0, stride)
    near_part0 = swap(near_side0)
    sent1 = side(act, far_tap, 1, [near_side0])
    came1 = inward(sent1)
    own0, own1, own2 = centre(act, taps, [0, 1, 2], [sent1])
    hg = hidden_grad(binned, out_weight, [own0])
    kept1, kept2 = keep(act, taps, [1, 2], stride, [hg[0]])
    grad0, hid0 = middle(
        [near_part0, far_part0], own0, 0, scale_mid, shift_mid, hg[0], [kept1]
    )
    near0 = swap(grad0)
    sent2 = side(act, far_tap, 2, [grad0])
    came2 = inward(sent2)
    joined1 = join(kept1, came1, [sent2])
    mids1 = swap(joined1)
    slope = slope_in(x, scale_in, shift_in, [joined1])
    total = back(None, [("own", 0, grad0), ("near", 0, near0)], taps, stride, [slope])
    joined2 = join(kept2, came2, [total])
    mids2 = swap(joined2)
    base = pooled_base(x, out_bias, [joined2])
    grad1, hid1 = middle([mids1], own1, 1, scale_mid, shift_mid, hg[1], [base])
    near1 = swap(grad1)
    far0 = outward(near0)
    grad2, hid2 = middle([mids2], own2, 2, scale_mid, shift_mid, hg[2], [grad1])
    near2 = swap(grad2)
    far2 = across(grad2)
    pooled, mean2 = pooled_out(base, [hid0, hid1, hid2], out_weight, batch)
    total = back(
        total,
        [("own", 1, grad1), ("own", 2, grad2), ("far", 0, far0)],
        taps,
        stride,
        [mean2],
    )
    near1, total = lax.optimization_barrier((near1, total))
    far1 = outward(near1)
    total = back(total, [("near", 1, near1), ("near", 2, near2)], taps, stride)
    settled = settle(total, [("far", 1, far1)], taps, slope, binned, stride)
    out = final(settled, [("far", 2, far2)], taps, slope, stride)
    return pooled, out.reshape(seqs_in.shape)


def solution(mesh):
    in_specs = (
        P("groups", "seq", None),
        P("groups", "seq", None),
        P(),
        P(),
        P(),
        P(),
        P(),
        P(),
        P(),
    )
    out_specs = (P("groups", "seq", None), P("groups", "seq", None))
    return jax.shard_map(local, mesh=mesh, in_specs=in_specs, out_specs=out_specs, check_vma=False)
```

```python
import functools

import jax
import jax.numpy as jnp
from jax import lax
from jax.experimental import pallas as pl
from jax.experimental.pallas import tpu as pltpu
from jax.sharding import PartitionSpec as P

DILATION_STEP = 512
BIN = 4
LANES = 128
AXIS = "seq"
GELU_COEF = 0.7978845608028654
F32 = jnp.float32
BF16 = jnp.bfloat16
SHARE = 64
TILES = 6
LIMIT = 12 * 1024 * 1024


def gelu_value(v):
    inner = jnp.tanh(v * (GELU_COEF + (GELU_COEF * 0.044715) * v * v))
    half = 0.5 * v
    return half + half * inner


def gelu_both(v):
    square = v * v
    inner = jnp.tanh(v * (GELU_COEF + (GELU_COEF * 0.044715) * square))
    half = 0.5 * v
    value = half + half * inner
    slope = (0.5 + 0.5 * inner) + half * (1.0 - inner * inner) * (
        GELU_COEF + (GELU_COEF * 0.134145) * square
    )
    return value, slope


def gelu_slope(v):
    return gelu_both(v)[1]


def dot_nn(a, b):
    return jnp.dot(a, b, preferred_element_type=F32)


def dot_nt(a, b):
    return lax.dot_general(a, b, (((1,), (1,)), ((), ())), preferred_element_type=F32)


def averaging(bins, rows):
    row = lax.broadcasted_iota(jnp.int32, (bins, rows), 0)
    column = lax.broadcasted_iota(jnp.int32, (bins, rows), 1)
    inside = (column >= row * BIN) & (column < row * BIN + BIN)
    return jnp.where(inside, 1.0 / BIN, 0.0).astype(BF16)


def spreading(rows, bins):
    row = lax.broadcasted_iota(jnp.int32, (rows, bins), 0)
    column = lax.broadcasted_iota(jnp.int32, (rows, bins), 1)
    inside = (row >= column * BIN) & (row < column * BIN + BIN)
    return jnp.where(inside, 1.0 / BIN, 0.0).astype(BF16)


def near_tap(stride):
    return 2 * lax.rem(lax.div(lax.axis_index(AXIS), stride), 2)


def cost_of(flops, nbytes, trans):
    return pl.CostEstimate(
        flops=flops // SHARE, bytes_accessed=nbytes // SHARE, transcendentals=trans // SHARE
    )


def local_call(body, name, operands, outs, cost, scratch=(), after=()):
    flops, nbytes, trans = cost
    single = not isinstance(outs, list)
    space = pl.BlockSpec(memory_space=pltpu.VMEM)
    if after:
        inner, skip = body, len(operands)
        body = lambda *refs: inner(*refs[:skip], *refs[skip + len(after) :])
        operands = [*operands, *after]
    shapes = [pltpu.VMEM(s, d) for s, d in ([outs] if single else outs)]
    return pl.pallas_call(
        body,
        name=name,
        in_specs=[space] * len(operands),
        out_specs=space if single else [space] * len(outs),
        out_shape=shapes[0] if single else shapes,
        scratch_shapes=list(scratch),
        compiler_params=pltpu.CompilerParams(vmem_limit_bytes=LIMIT),
        cost_estimate=cost_of(flops, nbytes, trans),
    )(*[pltpu.with_memory_space_constraint(v, pltpu.VMEM) for v in operands])

SPLITS = (256, 256, 256)


def bounds(n):
    return slice(sum(SPLITS[:n]), sum(SPLITS[: n + 1]))


def front_body(stride, x_hbm, s_hbm, b_hbm, w_hbm, x_ref, a_ref, p_ref, w_ref, s_ref, b_ref, sems):
    rows, width = x_ref.shape
    slabs = 4
    slab = rows // slabs
    copies = [
        pltpu.make_async_copy(s_hbm, s_ref, sems.at[0]),
        pltpu.make_async_copy(b_hbm, b_ref, sems.at[1]),
    ]
    copies += [
        pltpu.make_async_copy(
            x_hbm.at[pl.ds(n * slab, slab)], x_ref.at[pl.ds(n * slab, slab)], sems.at[2 + n]
        )
        for n in range(slabs)
    ]
    taps = pltpu.make_async_copy(w_hbm.at[near_tap(stride)], w_ref, sems.at[2 + slabs])
    for copy in copies:
        copy.start()
    taps.start()
    copies[0].wait()
    copies[1].wait()
    scale = s_ref[...].reshape(1, width)
    shift = b_ref[...].reshape(1, width)
    for n, copy in enumerate(copies[2:]):
        copy.wait()
        part = slice(n * slab, n * slab + slab)
        a_ref[part, :] = gelu_value(x_ref[part, :].astype(F32) * scale + shift).astype(BF16)
    taps.wait()
    p_ref[...] = dot_nn(a_ref[...], w_ref[:, bounds(0)]).astype(BF16)


def front(x, scale, shift, taps, stride):
    rows, width = x.shape
    mid = SPLITS[0]
    space = pl.BlockSpec(memory_space=pltpu.VMEM)
    far = pl.BlockSpec(memory_space=pltpu.HBM)
    operands = [pltpu.with_memory_space_constraint(v, pltpu.HBM) for v in (x, scale, shift, taps)]
    return pl.pallas_call(
        functools.partial(front_body, stride),
        name="front",
        in_specs=[far] * 4,
        out_specs=[space] * 3,
        out_shape=[
            pltpu.VMEM(x.shape, BF16),
            pltpu.VMEM((rows, width), BF16),
            pltpu.VMEM((rows, mid), BF16),
        ],
        scratch_shapes=[
            pltpu.VMEM(taps.shape[1:], BF16),
            pltpu.VMEM((width,), F32),
            pltpu.VMEM((width,), F32),
            pltpu.SemaphoreType.DMA((7,)),
        ],
        compiler_params=pltpu.CompilerParams(vmem_limit_bytes=LIMIT),
        cost_estimate=cost_of(2 * rows * width * mid, 2 * (x.size + taps.size), x.size),
    )(*operands)


def side_body(which, stride, a_ref, w_ref, o_ref):
    o_ref[...] = dot_nn(a_ref[...], w_ref[2 - near_tap(stride), :, bounds(which)]).astype(BF16)


def side(act, taps, which, stride, after=()):
    rows, width = act.shape
    return local_call(
        functools.partial(side_body, which, stride),
        "side",
        [act, taps],
        ((rows, SPLITS[which]), BF16),
        (2 * rows * width * SPLITS[which], 2 * rows * width, 0),
        after=after,
    )


def keep_body(stride, which, a_ref, w_ref, *outs):
    for n, out in zip(which, outs):
        out[...] = dot_nn(a_ref[...], w_ref[near_tap(stride), :, bounds(n)])


def keep(act, taps, which, stride, after=()):
    rows, width = act.shape
    return local_call(
        functools.partial(keep_body, stride, which),
        "keep",
        [act, taps],
        [((rows, SPLITS[n]), F32) for n in which],
        (2 * rows * width * sum(SPLITS[n] for n in which), 2 * rows * width, 0),
        after=after,
    )


def centre_body(which, a_ref, w_ref, *outs):
    for n, out in zip(which, outs):
        out[...] = dot_nn(a_ref[...], w_ref[1, :, bounds(n)])


def centre(act, taps, which, after):
    rows, width = act.shape
    return local_call(
        functools.partial(centre_body, which),
        "centre",
        [act, taps],
        [((rows, SPLITS[n]), F32) for n in which],
        (2 * rows * width * sum(SPLITS[n] for n in which), 2 * rows * width, 0),
        after=after,
    )


def join_body(k_ref, r_ref, o_ref):
    o_ref[...] = (k_ref[...] + r_ref[...].astype(F32)).astype(BF16)


def join(kept, came, after=()):
    return local_call(
        join_body,
        "join",
        [kept, came],
        (kept.shape, BF16),
        (kept.size, 8 * kept.size, 0),
        after=after,
    )


def hidden_grad_body(g_ref, w_ref, *outs):
    grad = (g_ref[...].astype(F32) * (1.0 / BIN)).astype(BF16)
    for n, out in enumerate(outs):
        out[...] = dot_nt(grad, w_ref[bounds(n), :])


def hidden_grad(binned, weight, after):
    bins, width = binned.shape
    mid = weight.shape[0]
    return local_call(
        hidden_grad_body,
        "hidden_grad",
        [binned, weight],
        [((bins, c), F32) for c in SPLITS],
        (2 * bins * width * mid, 2 * bins * width, 0),
        after=after,
    )


def middle_body(count, which, *refs):
    parts = refs[:count]
    p_ref, s_ref, b_ref, hg_ref, g_ref, h_ref, wide_ref = refs[count:]
    bins, width = hg_ref.shape
    for lane in range(width // LANES):
        columns = slice(lane * LANES, lane * LANES + LANES)
        for k in range(BIN):
            wide_ref[lane, pl.ds(k, bins, stride=BIN), :] = hg_ref[:, columns]
    first = bounds(which).start
    scales = s_ref[...].reshape(1, s_ref.shape[0])
    shifts = b_ref[...].reshape(1, b_ref.shape[0])
    for lane in range(width // LANES):
        columns = slice(lane * LANES, lane * LANES + LANES)
        among = slice(first + lane * LANES, first + lane * LANES + LANES)
        mid = p_ref[:, columns]
        for part in parts:
            mid = mid + part[:, columns].astype(F32)
        scale = scales[:, among]
        value, slope = gelu_both(mid * scale + shifts[:, among])
        g_ref[:, columns] = (wide_ref[lane] * slope * scale).astype(BF16)
        h_ref[:, columns] = value.astype(BF16)


def middle(parts, centre_part, which, scale, shift, hidden_grads, after=()):
    rows, mid = centre_part.shape
    return local_call(
        functools.partial(middle_body, len(parts), which),
        "middle",
        [*parts, centre_part, scale, shift, hidden_grads],
        [((rows, mid), BF16), ((rows, mid), BF16)],
        (30 * rows * mid, 12 * rows * mid, rows * mid),
        scratch=[pltpu.VMEM((mid // LANES, rows, LANES), F32)],
        after=after,
    )


def pooled_base_body(x_ref, b_ref, o_ref):
    bins, width = o_ref.shape
    average = averaging(bins, x_ref.shape[0])
    o_ref[...] = dot_nn(average, x_ref[...]) + b_ref[...].reshape(1, width)


def pooled_base(x, bias, after):
    rows, width = x.shape
    bins = rows // BIN
    return local_call(
        pooled_base_body,
        "pooled_base",
        [x, bias],
        ((bins, width), F32),
        (2 * bins * width * rows, 2 * rows * width, 0),
        after=after,
    )


def pooled_body(*refs):
    count = len(SPLITS)
    hidden = refs[:count]
    base_ref, w_ref, o_ref, mark_ref, out_ref, sem = refs[count:]
    bins, width = out_ref.shape
    rows = hidden[0].shape[0]
    average = averaging(bins, rows)
    total = base_ref[...]
    for n in range(count):
        mean = dot_nn(average, hidden[n][...]).astype(BF16)
        total = total + dot_nn(mean, w_ref[bounds(n), :])
    out_ref[...] = total.astype(BF16)
    mark_ref[...] = out_ref[:16, :LANES]
    half = bins // o_ref.shape[0]
    for n in range(o_ref.shape[0]):
        copy = pltpu.make_async_copy(out_ref.at[pl.ds(n * half, half)], o_ref.at[n], sem.at[n])
        copy.start()
    for n in range(o_ref.shape[0]):
        copy = pltpu.make_async_copy(out_ref.at[pl.ds(n * half, half)], o_ref.at[n], sem.at[n])
        copy.wait()


def pooled_out(base, hidden, weight, batch):
    bins, width = base.shape
    mid = weight.shape[0]
    operands = [*hidden, base, weight]
    return pl.pallas_call(
        pooled_body,
        name="pooled",
        in_specs=[pl.BlockSpec(memory_space=pltpu.VMEM)] * len(operands),
        out_specs=[pl.BlockSpec(memory_space=pltpu.HBM), pl.BlockSpec(memory_space=pltpu.VMEM)],
        out_shape=[
            pltpu.HBM((batch, bins // batch, width), BF16),
            pltpu.VMEM((16, LANES), BF16),
        ],
        scratch_shapes=[pltpu.VMEM((bins, width), BF16), pltpu.SemaphoreType.DMA((batch,))],
        compiler_params=pltpu.CompilerParams(vmem_limit_bytes=LIMIT),
        cost_estimate=cost_of(2 * bins * width * mid, 6 * bins * width, 0),
    )(*[pltpu.with_memory_space_constraint(v, pltpu.VMEM) for v in operands])


def slope_body(x_ref, s_ref, b_ref, o_ref):
    width = x_ref.shape[1]
    scale = s_ref[...].reshape(1, width)
    shift = b_ref[...].reshape(1, width)
    o_ref[...] = gelu_slope(x_ref[...].astype(F32) * scale + shift) * scale


def slope_in(x, scale, shift, after):
    return local_call(
        slope_body,
        "slope",
        [x, scale, shift],
        (x.shape, F32),
        (30 * x.size, 6 * x.size, x.size),
        after=after,
    )


def back_sum(stride, refs, kinds, w_ref, columns=slice(None)):
    near = near_tap(stride)
    taps = dict(own=1, near=near, far=2 - near, before=2, later=0)
    total = None
    for ref, (kind, n) in zip(refs, kinds):
        term = dot_nt(ref[...], w_ref[taps[kind], columns, bounds(n)])
        total = term if total is None else total + term
    return total


def back_body(stride, kinds, started, *refs):
    grads = refs[: len(kinds)]
    rest = refs[len(kinds) :]
    w_ref, o_ref = rest[0], rest[-1]
    total = back_sum(stride, grads, kinds, w_ref)
    o_ref[...] = rest[1][...] + total if started else total


def back(total, terms, taps, stride, after=()):
    kinds = [(kind, n) for kind, n, _ in terms]
    grads = [g for _, _, g in terms]
    rows = grads[0].shape[0]
    width = taps.shape[1]
    started = total is not None
    return local_call(
        functools.partial(back_body, stride, kinds, started),
        "back",
        [*grads, taps] + ([total] if started else []),
        ((rows, width), F32),
        (2 * rows * width * sum(g.shape[1] for g in grads), 8 * rows * width, 0),
        after=after,
    )


def touch_body(a_ref, b_ref, o_ref):
    o_ref[...] = a_ref[:16, :LANES] + b_ref[:16, :LANES]


def touch(a, b, after):
    return local_call(touch_body, "touch", [a, b], ((16, LANES), BF16), (1, 1, 0), after=after)


def settle_body(stride, kinds, *refs):
    grads = refs[: len(kinds)]
    c_ref, w_ref, d_ref, og_ref, o_ref = refs[len(kinds) :]
    spread = spreading(c_ref.shape[0], og_ref.shape[0])
    total = c_ref[...] + back_sum(stride, grads, kinds, w_ref)
    o_ref[...] = dot_nn(spread, og_ref[...]) + total * d_ref[...]


def settle(total, terms, taps, slope, binned, stride):
    kinds = [(kind, n) for kind, n, _ in terms]
    grads = [g for _, _, g in terms]
    rows, width = slope.shape
    return local_call(
        functools.partial(settle_body, stride, kinds),
        "settle",
        [*grads, total, taps, slope, binned],
        ((rows, width), F32),
        (2 * rows * width * sum(g.shape[1] for g in grads), 8 * rows * width, 0),
    )


def final_body(stride, kinds, tiles, *refs):
    grads = refs[: len(kinds)]
    c_ref, w_ref, d_ref, o_ref, out_ref, sems = refs[len(kinds) :]
    rows, width = c_ref.shape
    tile = width // tiles
    copies = []
    for n in range(tiles):
        columns = slice(n * tile, n * tile + tile)
        last = back_sum(stride, grads, kinds, w_ref, columns)
        out_ref[:, columns] = (c_ref[:, columns] + last * d_ref[:, columns]).astype(BF16)
        copy = pltpu.make_async_copy(out_ref.at[:, columns], o_ref.at[:, columns], sems.at[n])
        copy.start()
        copies.append(copy)
    for copy in copies:
        copy.wait()


def final(settled, terms, taps, slope, stride):
    kinds = [(kind, n) for kind, n, _ in terms]
    grads = [g for _, _, g in terms]
    rows, width = slope.shape
    tiles = TILES
    operands = [*grads, settled, taps, slope]
    return pl.pallas_call(
        functools.partial(final_body, stride, kinds, tiles),
        name="final",
        in_specs=[pl.BlockSpec(memory_space=pltpu.VMEM)] * len(operands),
        out_specs=pl.BlockSpec(memory_space=pltpu.HBM),
        out_shape=pltpu.HBM((rows, width), BF16),
        scratch_shapes=[pltpu.VMEM((rows, width), BF16), pltpu.SemaphoreType.DMA((tiles,))],
        compiler_params=pltpu.CompilerParams(vmem_limit_bytes=LIMIT),
        cost_estimate=cost_of(
            2 * rows * width * sum(g.shape[1] for g in grads), 8 * rows * width, 0
        ),
    )(*[pltpu.with_memory_space_constraint(v, pltpu.VMEM) for v in operands])


def local(
    seqs_in,
    pooled_grad,
    scale_in,
    shift_in,
    tap_weight_stack,
    scale_mid,
    shift_mid,
    out_weight,
    out_bias,
):
    batch, rows, width = seqs_in.shape
    count = lax.axis_size(AXIS)
    stride = DILATION_STEP // rows
    blocks = count // stride

    def hop(value, steps):
        return lax.ppermute(
            value, AXIS, [(i, i + steps) for i in range(count) if 0 <= i + steps < count]
        )

    def block_permute(value, move):
        pairs = []
        for b in range(blocks):
            to = move(b)
            if 0 <= to < blocks:
                pairs += [(b * stride + i, to * stride + i) for i in range(stride)]
        return lax.ppermute(value, AXIS, pairs)

    def swap(value):
        return block_permute(value, lambda b: b ^ 1)

    def across(value):
        return block_permute(value, lambda b: b + 1 if b % 2 else b - 1)

    def inward(value):
        return block_permute(value, lambda b: b + 2 if b % 2 else b - 2)

    def outward(value):
        return block_permute(value, lambda b: b - 2 if b % 2 else b + 2)

    flat = seqs_in.reshape(batch * rows, width)
    binned = pooled_grad.reshape(-1, width)
    x, act, kept0 = front(flat, scale_in, shift_in, tap_weight_stack, stride)
    taps, kept0 = lax.optimization_barrier((tap_weight_stack, kept0))
    near_part0 = swap(kept0)
    sent0 = side(act, taps, 0, stride)
    far_part0 = across(sent0)
    sent1 = side(act, taps, 1, stride, [sent0])
    came1 = inward(sent1)
    own0, own1, own2 = centre(act, taps, [0, 1, 2], [sent1])
    hg = hidden_grad(binned, out_weight, [own0])
    kept1, kept2 = keep(act, taps, [1, 2], stride, [hg[0]])
    arrived = touch(near_part0, sent1, [kept1])
    far_part0, arrived = lax.optimization_barrier((far_part0, arrived))
    grad0, hid0 = middle(
        [near_part0, far_part0], own0, 0, scale_mid, shift_mid, hg[0], [arrived]
    )
    near0 = swap(grad0)
    sent2 = side(act, taps, 2, stride, [grad0])
    came2 = inward(sent2)
    joined1 = join(kept1, came1, [sent2])
    mids1 = swap(joined1)
    slope = slope_in(x, scale_in, shift_in, [joined1])
    total = back(None, [("own", 0, grad0), ("near", 0, near0)], taps, stride, [slope])
    joined2 = join(kept2, came2, [total])
    mids2 = swap(joined2)
    base = pooled_base(x, out_bias, [joined2])
    grad1, hid1 = middle([mids1], own1, 1, scale_mid, shift_mid, hg[1], [base])
    near1 = swap(grad1)
    far0 = outward(near0)
    grad2, hid2 = middle([mids2], own2, 2, scale_mid, shift_mid, hg[2], [grad1])
    near2 = swap(grad2)
    far2 = across(grad2)
    pooled, mean2 = pooled_out(base, [hid0, hid1, hid2], out_weight, batch)
    total = back(
        total,
        [("own", 1, grad1), ("own", 2, grad2), ("far", 0, far0)],
        taps,
        stride,
        [mean2],
    )
    near1, total = lax.optimization_barrier((near1, total))
    far1 = outward(near1)
    total = back(total, [("near", 1, near1), ("near", 2, near2)], taps, stride)
    settled = settle(total, [("far", 1, far1)], taps, slope, binned, stride)
    out = final(settled, [("far", 2, far2)], taps, slope, stride)
    return pooled, out.reshape(seqs_in.shape)


def solution(mesh):
    in_specs = (
        P("groups", "seq", None),
        P("groups", "seq", None),
        P(),
        P(),
        P(),
        P(),
        P(),
        P(),
        P(),
    )
    out_specs = (P("groups", "seq", None), P("groups", "seq", None))
    return jax.shard_map(local, mesh=mesh, in_specs=in_specs, out_specs=out_specs, check_vma=False)
```
